32 devices in a mesh: tm: 8 (over z, x), state: 4 (over y, core).
Axes of the slice: x: 2, y: 2, z: 4, core: 2. Of those that a mesh axis runs over, the one named last changes fastest.
Arguments:
- dyn_cols: int32 [256, 8, 3], P('tm', 'state'), may hold values from 0 to 7, as said below
- dyn_vals: bfloat16 [256, 8, 64, 192], P('tm', 'state'), may hold values from -1 to 1
- obs_blocks: int32 [256, 2], P('tm'), may hold values from 0 to 7
- obs_op: bfloat16 [256, 64, 128], P('tm'), may hold values from -0.75 to 0.75
- obs_counts: int32 [256], P('tm'), may hold values from 32 to 128, as said below
- obs_values: float32 [256, 128], P('tm'), may hold values from -6 to 6
- gain: bfloat16 [256, 512, 128], P('tm', 'state'), may hold values from -0.0078125 to 0.0078125
- sources: float32 [256, 512], P('tm', 'state'), may hold values from -0.625 to 0.625
- prior: float32 [512], replicated, may hold values from -6 to 6
Outputs:
- filtered: float32 [256, 512], P('tm', 'state')
The draws below stay inside these ranges and needn't reach their ends.
Inputs may be any that keep to these rules, and one draw needn't show every extreme that they name: `dyn_cols`: for every step and block row i, the first entry is i itself and the 3 entries are distinct block columns. `obs_counts`: some step has all 128 observations present.
All inputs are finite; a program needn't handle non-finite values.
Results may differ from the reference program's by a relative error of at most 0.0003.
The reference program's roundings to bfloat16 on the way count: a program that leaves them out, or rounds other values in their place, can miss the bound.
Values may be sent and summed in bfloat16 or wider, within the bound.
No kernel may reach another device: no remote copies, remote signals or barrier semaphores. Data moves between devices by JAX's collectives and lax.ppermute only.
A program may use at most 128 MiB of HBM per device.

```python
import math
import jax
import jax.numpy as jnp
from jax import lax

NS = 512
BS = 64
KF = 3
OBS = 128
NB = 8
OB = 2
HORIZON_LENGTH = 256


def draw_dyn_cols(key, part):
    scores = jax.random.randint(key, (HORIZON_LENGTH, NB, NB - 1), 0, 1 << 20) * NB + jnp.arange(NB - 1)
    picked = lax.top_k(scores, KF - 1)[1] + 1
    row_index = jnp.arange(NB)[None, :, None]
    others = (row_index + picked) % NB
    leading = jnp.broadcast_to(row_index, (HORIZON_LENGTH, NB, 1))
    return jnp.concatenate([leading, others], axis=2).astype(jnp.int32)


def draw_dyn_vals(key, part):
    quick_decay_seed, speed_seed, layer_level_seed, spike_seed, decay_seed, perturbation_seed = jax.random.split(key, 6)
    share = 0.25
    fast = jax.random.uniform(quick_decay_seed, (NB, BS)) < share
    fast_rate = jnp.exp(-jax.random.uniform(speed_seed, (NB, BS), minval=1.0 / 50.0, maxval=1.0 / 30.0))
    depth = jax.random.uniform(layer_level_seed, (HORIZON_LENGTH, NB, BS), minval=0.25, maxval=1.25)
    gradual_decay_speed = 1.0 - 0.002 * depth
    spike_location = jax.random.randint(spike_seed, (2,), 0, HORIZON_LENGTH)
    spike_struck_flags = jnp.any(jnp.arange(HORIZON_LENGTH)[:, None] == spike_location[None, :], axis=1)
    decay_factor = jax.random.uniform(decay_seed, (HORIZON_LENGTH, NB, BS), minval=0.5, maxval=0.8)
    gradual_decay_speed = jnp.where(spike_struck_flags[:, None, None], gradual_decay_speed * decay_factor, gradual_decay_speed)
    rate = jnp.where(fast[None, :, :], fast_rate[None, :, :], gradual_decay_speed)
    diagonal = rate[..., None] * jnp.eye(BS, dtype=jnp.float32)
    padding = jnp.zeros((HORIZON_LENGTH, NB, BS, (KF - 1) * BS), jnp.float32)
    leading = jnp.concatenate([diagonal, padding], axis=3)
    off_diag = 1.0 - jnp.concatenate([jnp.eye(BS, dtype=jnp.float32), jnp.zeros((BS, (KF - 1) * BS), jnp.float32)], axis=1)
    noise = jax.random.truncated_normal(perturbation_seed, -4.0, 4.0, (HORIZON_LENGTH, NB, BS, KF * BS)) * (0.014 / math.sqrt(KF * BS))
    return (leading + noise * off_diag).astype(jnp.bfloat16)


def draw_obs_counts(key, part):
    key_count, key_where = jax.random.split(key, 2)
    counts = jax.random.randint(key_count, (HORIZON_LENGTH,), OBS // 4, OBS + 1)
    where_full = jax.random.randint(key_where, (), 0, HORIZON_LENGTH)
    return jnp.where(jnp.arange(HORIZON_LENGTH) == where_full, OBS, counts).astype(jnp.int32)


def plant(drawn, own_key, low, top_value):
    dims = drawn.shape
    index_at = [jax.random.randint(jax.random.fold_in(own_key, axis), (), 0, dims[axis]) for axis in range(len(dims))]
    drawn = drawn.at[tuple(index_at)].set(low)
    longest = dims.index(max(dims))
    index_at[longest] = (index_at[longest] + 1) % dims[longest]
    return drawn.at[tuple(index_at)].set(top_value)


def block_levels(key, extent, shards, smallest, high):
    level, own = 1.0, jax.random.fold_in(key, 6)
    for position, shards_of in shards:
        steps = jnp.exp(jax.random.uniform(jax.random.fold_in(own, position), (shards_of,), jnp.float32, smallest / len(shards), high / len(shards)))
        level = level * jnp.repeat(steps, extent[position] // shards_of).reshape([-1 if axis == position else 1 for axis in range(len(extent))])
    return level


def scatter_about(own_key, shape, deviation, most, shards=(), kind=jnp.bfloat16):
    result = jax.random.normal(own_key, shape, jnp.float32) * deviation
    if len(shards) > 0:
        result = block_levels(own_key, shape, shards, -0.22, 0.18) * result
    return jnp.clip(result, min=-most, max=most).astype(kind)


def setup_inputs(seed: int = 0) -> dict:
    key_of = jax.random.split(jax.random.key(seed), 10)
    return {
        "dyn_cols": draw_dyn_cols(jax.random.fold_in(key_of[9], 71), 0),
        "dyn_vals": draw_dyn_vals(jax.random.fold_in(key_of[9], 71), 0),
        "obs_blocks": plant(jax.random.randint(key_of[2], (HORIZON_LENGTH, OB), 0, NB), jax.random.fold_in(key_of[2], 1), 0, NB - 1).astype(jnp.int32),
        "obs_op": scatter_about(key_of[3], (HORIZON_LENGTH, BS, OBS), BS ** -0.5, 0.75, ((0, 8),)),
        "obs_counts": draw_obs_counts(jax.random.fold_in(key_of[9], 71), 0),
        "obs_values": scatter_about(key_of[5], (HORIZON_LENGTH, OBS), 1.0, 6.0, ((0, 8),), jnp.float32),
        "gain": scatter_about(key_of[6], (HORIZON_LENGTH, NS, OBS), (4000 * OBS) ** -0.5, 0.0078125, ((0, 8), (1, 4))),
        "sources": scatter_about(key_of[7], (HORIZON_LENGTH, NS), 0.04, 0.625, ((0, 8), (1, 4)), jnp.float32),
        "prior": scatter_about(key_of[8], (NS,), 1.0, 6.0, (), jnp.float32),
    }


HIGHEST = lax.Precision.HIGHEST


def assemble(columns, values):
    count_rows = columns.shape[0]
    onehot = (columns[:, :, None] == jnp.arange(NB)[None, None, :]).astype(jnp.float32)
    blocks = values.reshape(count_rows, BS, KF, BS).astype(jnp.float32)
    assembled = jnp.einsum('rkc,rakb->racb', onehot, blocks, precision=HIGHEST)
    return assembled.reshape(count_rows * BS, NS)


def reference(dyn_cols, dyn_vals, obs_blocks, obs_op, obs_counts, obs_values, gain, sources, prior):
    def advance(state_mean, inputs):
        columns, values, observed, operator, count, measured, gain_step, source = inputs
        forward = assemble(columns, values)
        selected = forward.reshape(NB, BS, NS)[observed]
        source_blocks = source.reshape(NB, BS)[observed]
        operator_blocks = operator.reshape(BS, OB, BS).astype(jnp.float32)
        image = jnp.einsum('boa,obn->oan', operator_blocks, selected, precision=HIGHEST)
        image = image.reshape(OBS, NS).astype(jnp.bfloat16)
        source_image = jnp.einsum('boa,ob->oa', operator_blocks, source_blocks, precision=HIGHEST)
        source_image = source_image.reshape(OBS).astype(jnp.bfloat16)
        active = jnp.arange(OBS) < count
        masked = jnp.where(active[:, None], image, jnp.zeros((), jnp.bfloat16))
        innovation = jnp.where(active, measured - lax.optimization_barrier(source_image).astype(jnp.float32), 0.0)
        correction = jnp.dot(gain_step, masked, preferred_element_type=jnp.float32)
        element = (forward - correction).astype(jnp.bfloat16)
        offset = source + jnp.dot(gain_step.astype(jnp.float32), innovation, precision=HIGHEST)
        new_mean = jnp.dot(element.astype(jnp.float32), state_mean, precision=HIGHEST) + offset
        return new_mean, new_mean

    _, filtered = lax.scan(advance, prior, (dyn_cols, dyn_vals, obs_blocks, obs_op, obs_counts, obs_values, gain, sources))
    return filtered
```

```python
import functools

import jax
import jax.numpy as jnp
from jax import lax
from jax.experimental import pallas as pl
from jax.experimental.pallas import tpu as pltpu
from jax.sharding import PartitionSpec as P

BF = jnp.bfloat16
F32 = jnp.float32
VMEM_LIMIT = 60 * 1024 * 1024
ROWS = 16


def nt(a, b):
    return lax.dot_general(a, b, (((1,), (1,)), ((), ())), preferred_element_type=F32)


def nn(a, b):
    return lax.dot_general(a, b, (((1,), (0,)), ((), ())), preferred_element_type=F32)


def tn(a, b):
    return lax.dot_general(a, b, (((0,), (0,)), ((), ())), preferred_element_type=F32)


def split3(row):
    hi = row.astype(BF).astype(F32)
    rest = row - hi
    mid = rest.astype(BF).astype(F32)
    low = rest - mid
    at = lax.broadcasted_iota(jnp.int32, (ROWS, row.shape[1]), 0)
    zero = jnp.zeros((), F32)
    return jnp.where(at == 0, hi, jnp.where(at == 1, mid, jnp.where(at == 2, low, zero))).astype(BF)


def fold(rows):
    return jnp.sum(rows, axis=0, keepdims=True)


def vmem(n):
    return [pl.BlockSpec(memory_space=pltpu.VMEM)] * n


def pack_kernel(parts, pairs, bs, s_ref, *refs):
    vals, gains, outs = refs[:parts], refs[parts : 2 * parts], refs[2 * parts :]
    for d in range(parts):
        for q in range(pairs):
            base = 0
            for i in range(2):
                outs[d][0, q, i * bs : (i + 1) * bs, :] = vals[d][0, 2 * q + i, :, : 2 * bs]
            base = 2 * bs
            third = jnp.concatenate(
                [vals[d][0, 2 * q, :, 2 * bs :], vals[d][0, 2 * q + 1, :, 2 * bs :]], axis=1
            )
            outs[d][0, q, base : base + bs, :] = third
            base = 3 * bs
            outs[d][0, q, base : base + 2 * bs, :] = gains[d][0, q * 2 * bs : (q + 1) * 2 * bs, :]


def pack(position, dyn_vals, gain, parts, chunk, first, count):
    steps, lb, bs, width = dyn_vals.shape
    rows, obs = gain.shape[1:]
    pairs = lb // 2

    def from_part(d, trail):
        return lambda j, s: ((s[0] ^ d) * chunk + first + j,) + (0,) * trail

    shape = (count, pairs, 5 * bs, 2 * bs)
    return pl.pallas_call(
        functools.partial(pack_kernel, parts, pairs, bs),
        grid_spec=pltpu.PrefetchScalarGridSpec(
            num_scalar_prefetch=1,
            grid=(count,),
            in_specs=[pl.BlockSpec((1, lb, bs, width), from_part(d, 3)) for d in range(parts)]
            + [pl.BlockSpec((1, rows, obs), from_part(d, 2)) for d in range(parts)],
            out_specs=[pl.BlockSpec((1,) + shape[1:], lambda j, s: (j, 0, 0, 0))] * parts,
        ),
        out_shape=[jax.ShapeDtypeStruct(shape, BF)] * parts,
        name=f"pack_{first}",
    )(position, *([dyn_vals] * parts), *([gain] * parts))


def chunk_kernel(
    parts, pairs, bs, chunk, first, count, s_ref, tm_ref, blocks_ref, counts_ref, *refs
):
    cols = refs[:parts]
    refs = refs[parts:]
    data, small = refs[:parts], refs[parts : 2 * parts]
    op_ref, values_ref, prior_ref, hi_in, lo_in, vec_in = refs[2 * parts : 2 * parts + 6]
    elements, offsets, hi_ref, lo_ref, vec_ref = refs[2 * parts + 6 : 2 * parts + 11]
    dyn, gains, source, chosen = refs[2 * parts + 11 :]
    s = s_ref[0]
    ns = parts * pairs * 2 * bs
    lane = lax.broadcasted_iota(jnp.int32, (bs, 2 * bs), 1)
    left = lane < bs
    lane_row = lax.broadcasted_iota(jnp.int32, (1, 2 * bs), 1)
    slot = lax.broadcasted_iota(jnp.int32, (2 * bs, 1), 0)
    for d in range(parts):
        for q in range(pairs):
            source[(s ^ d) * pairs + q] = small[d][:, q * 2 * bs : (q + 1) * 2 * bs]
    for j in range(count):
        here = first + j
        k = s * chunk + here
        for d in range(parts):
            for q in range(pairs):
                group = (s ^ d) * pairs + q
                gains[pl.ds(pl.multiple_of(group * 2 * bs, 2 * bs), 2 * bs), :] = data[d][
                    j, q, 3 * bs : 5 * bs, :
                ]
                third = data[d][j, q, 2 * bs : 3 * bs, :].astype(F32)
                third_turned = pltpu.roll(third, bs, 1)
                for i in range(2):
                    both = data[d][j, q, i * bs : (i + 1) * bs, :].astype(F32)
                    both_turned = pltpu.roll(both, bs, 1)
                    lefts = (both, both_turned, third if i == 0 else third_turned)
                    rights = (both_turned, both, third_turned if i == 0 else third)
                    where = [cols[d][here, (2 * q + i) * 3 + e] for e in range(3)]
                    row = pl.multiple_of(group * 2 * bs + i * bs, bs)
                    for tile in range(parts * pairs):
                        value_l = jnp.zeros((bs, 2 * bs), F32)
                        value_r = jnp.zeros((bs, 2 * bs), F32)
                        for e in range(3):
                            value_l = jnp.where(where[e] == 2 * tile, lefts[e], value_l)
                            value_r = jnp.where(where[e] == 2 * tile + 1, rights[e], value_r)
                        dyn[pl.ds(row, bs), tile * 2 * bs : (tile + 1) * 2 * bs] = jnp.where(
                            left, value_l, value_r
                        ).astype(BF)
        operator = op_ref[k].astype(F32)
        diagonal = jnp.concatenate(
            [jnp.where(left, operator, 0.0), jnp.where(left, 0.0, operator)], axis=0
        ).astype(BF)
        picks = []
        for o in range(2):
            block = blocks_ref[k, o]
            chosen[o * bs : (o + 1) * bs, :] = dyn[pl.ds(pl.multiple_of(block * bs, bs), bs), :]
            row = source[block // 2, pl.ds(here, 1), :]
            turned = pltpu.roll(row, bs, 1)
            picks.append(jnp.where(block % 2 == o, row, turned))
        image = tn(diagonal, chosen[...])
        masked = jnp.where(slot < counts_ref[k], image, 0.0).astype(BF)
        pick = jnp.where(lane_row < bs, picks[0], picks[1])
        source_image = fold(nn(split3(pick), diagonal)).astype(BF).astype(F32)
        innovation = jnp.where(
            lane_row < counts_ref[k], values_ref[pl.ds(k, 1), :] - source_image, 0.0
        )
        shift = fold(nt(split3(innovation), gains[...]))
        shift = shift + jnp.concatenate(
            [source[g, pl.ds(here, 1), :] for g in range(parts * pairs)], axis=1
        )
        offsets[j] = jnp.broadcast_to(shift, (8, ns))
        for g in range(parts * pairs):
            rows = slice(g * 2 * bs, (g + 1) * 2 * bs)
            elements[j, rows, :] = (
                dyn[rows, :].astype(F32) - nn(gains[rows, :], masked)
            ).astype(BF)
    if first == 0:
        begin = jnp.logical_and(s == 0, tm_ref[0] == 0)
        vec = jnp.where(begin, prior_ref[...], 0.0)
    else:
        vec = vec_in[0:1, :]
    step_rows = 256 if ns % 256 == 0 else ns
    for j in range(count):
        element = elements[j]
        vec = fold(nt(split3(vec), element)) + offsets[j, 0:1, :]
        for r in range(0, ns, step_rows):
            rows = slice(r, r + step_rows)
            if first == 0 and j == 0:
                across = lax.broadcasted_iota(jnp.int32, (step_rows, ns), 1)
                down = lax.broadcasted_iota(jnp.int32, (step_rows, ns), 0) + r
                unit = jnp.where(across == down, 1.0, 0.0).astype(BF)
                hi_ref[rows, :] = nt(unit, element).astype(BF)
                lo_ref[rows, :] = jnp.zeros((step_rows, ns), BF)
                continue
            if j == 0:
                hi, lo = hi_in[rows, :], lo_in[rows, :]
            else:
                hi, lo = hi_ref[rows, :], lo_ref[rows, :]
            if first == 0 and j == 1:
                moved = nt(hi, element)
            else:
                moved = nt(hi, element) + nt(lo, element)
            top = moved.astype(BF)
            hi_ref[rows, :] = top
            lo_ref[rows, :] = (moved - top.astype(F32)).astype(BF)
    vec_ref[...] = jnp.broadcast_to(vec, (8, ns))


def chunk_piece(
    position, span, cols, blocks, counts, data, small, obs_op, obs_values, prior, state, first, count
):
    parts = len(data)
    pairs, height, width = data[0].shape[1:]
    bs = width // 2
    ns = parts * pairs * width
    chunk = small[0].shape[0]
    if state is None:
        state = (jnp.zeros((8, 128), BF), jnp.zeros((8, 128), BF), jnp.zeros((8, 128), F32))
    return pl.pallas_call(
        functools.partial(chunk_kernel, parts, pairs, bs, chunk, first, count),
        grid_spec=pltpu.PrefetchScalarGridSpec(
            num_scalar_prefetch=4 + parts,
            grid=(),
            in_specs=vmem(2 * parts + 6),
            out_specs=vmem(5),
            scratch_shapes=[
                pltpu.VMEM((ns, ns), BF),
                pltpu.VMEM((ns, width), BF),
                pltpu.VMEM((parts * pairs, chunk, width), F32),
                pltpu.VMEM((width, ns), BF),
            ],
        ),
        out_shape=[
            jax.ShapeDtypeStruct((count, ns, ns), BF),
            jax.ShapeDtypeStruct((count, 8, ns), F32),
            jax.ShapeDtypeStruct((ns, ns), BF),
            jax.ShapeDtypeStruct((ns, ns), BF),
            jax.ShapeDtypeStruct((8, ns), F32),
        ],
        compiler_params=pltpu.CompilerParams(vmem_limit_bytes=VMEM_LIMIT),
        name=f"chunk_{first}",
    )(position, span, blocks, counts, *cols, *data, *small, obs_op, obs_values, prior, *state)


def apply_map(row, hi, lo):
    parts = split3(row)
    return fold(nn(parts, hi) + nn(parts, lo))


def join_maps(one, two, hi_ref, lo_ref, vec_ref):
    ns = hi_ref.shape[0]
    step = 256 if ns % 256 == 0 else ns
    for r in range(0, ns, step):
        rows = slice(r, r + step)
        product = nn(one[0][rows, :], two[0][...]) + (
            nn(one[0][rows, :], two[1][...]) + nn(one[1][rows, :], two[0][...])
        )
        top = product.astype(BF)
        hi_ref[rows, :] = top
        lo_ref[rows, :] = (product - top.astype(F32)).astype(BF)
    vec = apply_map(one[2][0:1, :], two[0][...], two[1][...]) + two[2][0:1, :]
    vec_ref[...] = jnp.broadcast_to(vec, vec_ref.shape)


def pair_kernel(bit, s_ref, *refs):
    own, other, out = refs[:3], refs[3:6], refs[6:9]
    halves = refs[9:11]
    earlier = (s_ref[0] & bit) == 0

    @pl.when(earlier)
    def _():
        join_maps(own, other, *out)

    @pl.when(jnp.logical_not(earlier))
    def _():
        join_maps(other, own, *out)

    half = out[0].shape[0] // 2
    start = pl.multiple_of((s_ref[0] & 1) * half, half)
    halves[0][...] = out[0][pl.ds(start, half), :]
    halves[1][...] = out[1][pl.ds(start, half), :]


def join_pair(position, own, other, bit):
    ns = own[0].shape[0]
    return pl.pallas_call(
        functools.partial(pair_kernel, bit),
        grid_spec=pltpu.PrefetchScalarGridSpec(
            num_scalar_prefetch=1, grid=(), in_specs=vmem(6), out_specs=vmem(5)
        ),
        out_shape=[
            jax.ShapeDtypeStruct((ns, ns), BF),
            jax.ShapeDtypeStruct((ns, ns), BF),
            jax.ShapeDtypeStruct((8, ns), F32),
            jax.ShapeDtypeStruct((ns // 2, ns), BF),
            jax.ShapeDtypeStruct((ns // 2, ns), BF),
        ],
        compiler_params=pltpu.CompilerParams(vmem_limit_bytes=VMEM_LIMIT),
        name=f"join_{bit}",
    )(position, *own, *other)


def wide_kernel(bit, s_ref, *refs):
    own, near, far, vec_other = refs[:3], refs[3:5], refs[5:7], refs[7]
    out, other = refs[8:11], refs[11:13]
    half = own[0].shape[0] // 2
    start = pl.multiple_of((s_ref[0] & 1) * half, half)
    rest = pl.multiple_of(half - (s_ref[0] & 1) * half, half)
    for i in range(2):
        other[i][pl.ds(start, half), :] = near[i][...]
        other[i][pl.ds(rest, half), :] = far[i][...]
    earlier = (s_ref[0] & bit) == 0

    @pl.when(earlier)
    def _():
        join_maps(own, (other[0], other[1], vec_other), *out)

    @pl.when(jnp.logical_not(earlier))
    def _():
        join_maps((other[0], other[1], vec_other), own, *out)


def join_wide(position, own, near, far, vec_other, bit):
    ns = own[0].shape[0]
    whole = jax.ShapeDtypeStruct((ns, ns), BF)
    return pl.pallas_call(
        functools.partial(wide_kernel, bit),
        grid_spec=pltpu.PrefetchScalarGridSpec(
            num_scalar_prefetch=1, grid=(), in_specs=vmem(8), out_specs=vmem(5)
        ),
        out_shape=[whole, whole, jax.ShapeDtypeStruct((8, ns), F32), whole, whole],
        compiler_params=pltpu.CompilerParams(vmem_limit_bytes=VMEM_LIMIT),
        name=f"join_{bit}",
    )(position, *own, *near, *far, vec_other)


def hop_kernel(row_ref, hi_ref, lo_ref, vec_ref, out_ref):
    out_ref[...] = apply_map(row_ref[...], hi_ref[...], lo_ref[...]) + vec_ref[0:1, :]


def hop(row, hi, lo, vec):
    return pl.pallas_call(
        hop_kernel,
        in_specs=vmem(4),
        out_specs=vmem(1)[0],
        out_shape=jax.ShapeDtypeStruct(row.shape, F32),
        name="hop",
    )(row, hi, lo, vec)


def sweep_kernel(levels, pieces, parts, s_ref, tm_ref, *refs):
    row_ref, prior_ref = refs[:2]
    maps = [refs[2 + 3 * n : 5 + 3 * n] for n in range(levels)]
    refs = refs[2 + 3 * levels :]
    elements, offsets = refs[:pieces], refs[pieces : 2 * pieces]
    outs = refs[2 * pieces : 2 * pieces + parts]
    current_ref, spread = refs[2 * pieces + parts :]
    s = s_ref[0]
    begin = jnp.logical_and(s == 0, tm_ref[0] == 0)
    current_ref[...] = row_ref[...] + jnp.where(begin, prior_ref[...], 0.0)
    for n in reversed(range(levels)):
        hi, lo, vec = maps[n]

        @pl.when((s & (1 << n)) != 0)
        def _():
            current_ref[...] = apply_map(current_ref[...], hi[...], lo[...]) + vec[0:1, :]

    current = current_ref[...]
    at = 0
    width = spread.shape[2]
    for p in range(pieces):
        for j in range(elements[p].shape[0]):
            current = fold(nt(split3(current), elements[p][j])) + offsets[p][j, 0:1, :]
            for d in range(parts):
                spread[d, at : at + 1, :] = current[:, d * width : (d + 1) * width]
            at += 1
    for d in range(parts):
        outs[d][...] = spread[s ^ d]


def sweep(position, span, row, prior, maps, elements, offsets, parts):
    ns = row.shape[1]
    levels, pieces = len(maps), len(elements)
    chunk = sum(e.shape[0] for e in elements)
    width = ns // parts
    return pl.pallas_call(
        functools.partial(sweep_kernel, levels, pieces, parts),
        grid_spec=pltpu.PrefetchScalarGridSpec(
            num_scalar_prefetch=2,
            grid=(),
            in_specs=vmem(2 + 3 * levels + 2 * pieces),
            out_specs=vmem(parts),
            scratch_shapes=[
                pltpu.VMEM((1, ns), F32),
                pltpu.VMEM((parts, chunk, width), F32),
            ],
        ),
        out_shape=[jax.ShapeDtypeStruct((chunk, width), F32)] * parts,
        compiler_params=pltpu.CompilerParams(vmem_limit_bytes=VMEM_LIMIT),
        name="sweep",
    )(position, span, row, prior, *[m for trio in maps for m in trio], *elements, *offsets)


def body(dyn_cols, dyn_vals, obs_blocks, obs_op, obs_counts, obs_values, gain, sources, prior):
    steps, lb, bs, width = dyn_vals.shape
    parts = lax.axis_size("state")
    spans = lax.axis_size("tm")
    chunk = steps // parts
    ns = prior.shape[0]
    s = lax.axis_index("state")
    t = lax.axis_index("tm")
    position = s.reshape(1).astype(jnp.int32)
    span = t.reshape(1).astype(jnp.int32)
    prior_row = prior.reshape(1, ns)

    def across(x, d):
        return lax.ppermute(x, "state", [(i, i ^ d) for i in range(parts)])

    order = sorted(range(1, parts), reverse=True)
    table = jnp.concatenate(
        [sources, dyn_cols.reshape(steps, -1).astype(F32)], axis=1
    ).reshape(parts, chunk, -1)
    small = [lax.dynamic_index_in_dim(table, s ^ d, 0, False) for d in range(parts)]
    small = [small[0]] + [across(small[d], d) for d in range(1, parts)]
    cols = [x[:, lb * bs :].astype(jnp.int32) for x in small]
    small = [x[:, : lb * bs] for x in small]

    per = 2 if chunk % 2 == 0 else 1
    state = None
    elements, offsets = [], []
    for first in range(0, chunk, per):
        packed = pack(position, dyn_vals, gain, parts, chunk, first, per)
        arrived = {d: across(packed[d], d) for d in order}
        data = [packed[0]] + [arrived[d] for d in range(1, parts)]
        element, offset, *state = chunk_piece(
            position, span, cols, obs_blocks, obs_counts, data, small, obs_op, obs_values,
            prior_row, state, first, per,
        )
        elements.append(element)
        offsets.append(offset)

    maps = []
    bit = 1
    while bit < parts:
        if bit == 1:
            other = [across(x, bit) for x in state]
            maps.append(other)
            *state, half_hi, half_lo = join_pair(position, state, other, bit)
        else:
            near = [across(half_hi, bit), across(half_lo, bit)]
            vec_other = across(state[2], bit)
            far = [across(x, 1) for x in near]
            *state, other_hi, other_lo = join_wide(position, state, near, far, vec_other, bit)
            maps.append([other_hi, other_lo, vec_other])
        bit *= 2

    current = state[2][0:1, :]
    entry = jnp.zeros((1, ns), F32)
    for h in range(spans - 1):
        arriving = lax.ppermute(current, "tm", [(h, h + 1)])
        entry = entry + arriving
        current = hop(arriving, *state)

    mine = sweep(position, span, entry, prior_row, maps, elements, offsets, parts)
    got = [mine[0]] + [across(mine[d], d) for d in range(1, parts)]
    bit = 1
    while bit < parts:
        swapped = [got[d ^ bit] for d in range(parts)]
        got = [jnp.where((s & bit) != 0, b, a) for a, b in zip(got, swapped)]
        bit *= 2
    return jnp.concatenate(got, axis=0)


def solution(mesh):
    return jax.shard_map(
        body,
        mesh=mesh,
        in_specs=(
            P("tm", "state", None),
            P("tm", "state", None, None),
            P("tm", None),
            P("tm", None, None),
            P("tm"),
            P("tm", None),
            P("tm", "state", None),
            P("tm", "state"),
            P(),
        ),
        out_specs=P("tm", "state"),
        check_vma=False,
    )
```

```python
import functools

import jax
import jax.numpy as jnp
from jax import lax
from jax.experimental import pallas as pl
from jax.experimental.pallas import tpu as pltpu
from jax.sharding import PartitionSpec as P

BF = jnp.bfloat16
F32 = jnp.float32
VMEM_LIMIT = 20 * 1024 * 1024
ROWS = 16


def nt(a, b):
    return lax.dot_general(a, b, (((1,), (1,)), ((), ())), preferred_element_type=F32)


def nn(a, b):
    return lax.dot_general(a, b, (((1,), (0,)), ((), ())), preferred_element_type=F32)


def tn(a, b):
    return lax.dot_general(a, b, (((0,), (0,)), ((), ())), preferred_element_type=F32)


def split3(row):
    hi = row.astype(BF).astype(F32)
    rest = row - hi
    mid = rest.astype(BF).astype(F32)
    low = rest - mid
    at = lax.broadcasted_iota(jnp.int32, (ROWS, row.shape[1]), 0)
    zero = jnp.zeros((), F32)
    return jnp.where(at == 0, hi, jnp.where(at == 1, mid, jnp.where(at == 2, low, zero))).astype(BF)


def fold(rows):
    return jnp.sum(rows, axis=0, keepdims=True)


def vmem(n):
    return [pl.BlockSpec(memory_space=pltpu.VMEM)] * n


def pack_kernel(parts, pairs, bs, s_ref, *refs):
    vals, gains, outs = refs[:parts], refs[parts : 2 * parts], refs[2 * parts :]
    for d in range(parts):
        for q in range(pairs):
            base = 0
            for i in range(2):
                outs[d][0, q, i * bs : (i + 1) * bs, :] = vals[d][0, 2 * q + i, :, : 2 * bs]
            base = 2 * bs
            third = jnp.concatenate(
                [vals[d][0, 2 * q, :, 2 * bs :], vals[d][0, 2 * q + 1, :, 2 * bs :]], axis=1
            )
            outs[d][0, q, base : base + bs, :] = third
            base = 3 * bs
            outs[d][0, q, base : base + 2 * bs, :] = gains[d][0, q * 2 * bs : (q + 1) * 2 * bs, :]


def pack(position, dyn_vals, gain, parts, chunk, first, count):
    steps, lb, bs, width = dyn_vals.shape
    rows, obs = gain.shape[1:]
    pairs = lb // 2

    def from_part(d, trail):
        return lambda j, s: ((s[0] ^ d) * chunk + first + j,) + (0,) * trail

    shape = (count, pairs, 5 * bs, 2 * bs)
    return pl.pallas_call(
        functools.partial(pack_kernel, parts, pairs, bs),
        grid_spec=pltpu.PrefetchScalarGridSpec(
            num_scalar_prefetch=1,
            grid=(count,),
            in_specs=[pl.BlockSpec((1, lb, bs, width), from_part(d, 3)) for d in range(parts)]
            + [pl.BlockSpec((1, rows, obs), from_part(d, 2)) for d in range(parts)],
            out_specs=[pl.BlockSpec((1,) + shape[1:], lambda j, s: (j, 0, 0, 0))] * parts,
        ),
        out_shape=[jax.ShapeDtypeStruct(shape, BF)] * parts,
        compiler_params=pltpu.CompilerParams(vmem_limit_bytes=VMEM_LIMIT),
        name=f"pack_{first}",
    )(position, *([dyn_vals] * parts), *([gain] * parts))


def chunk_kernel(
    parts, pairs, bs, chunk, first, count, s_ref, tm_ref, blocks_ref, counts_ref, *refs
):
    cols = refs[:parts]
    refs = refs[parts:]
    data, small = refs[:parts], refs[parts : 2 * parts]
    op_ref, values_ref, prior_ref, hi_in, lo_in, vec_in = refs[2 * parts : 2 * parts + 6]
    elements, offsets, hi_ref, lo_ref, vec_ref = refs[2 * parts + 6 : 2 * parts + 11]
    dyn, gains, source, chosen = refs[2 * parts + 11 :]
    s = s_ref[0]
    ns = parts * pairs * 2 * bs
    lane = lax.broadcasted_iota(jnp.int32, (bs, 2 * bs), 1)
    left = lane < bs
    lane_row = lax.broadcasted_iota(jnp.int32, (1, 2 * bs), 1)
    slot = lax.broadcasted_iota(jnp.int32, (2 * bs, 1), 0)
    for d in range(parts):
        for q in range(pairs):
            source[(s ^ d) * pairs + q] = small[d][:, q * 2 * bs : (q + 1) * 2 * bs]
    for j in range(count):
        here = first + j
        k = s * chunk + here
        for d in range(parts):
            for q in range(pairs):
                group = (s ^ d) * pairs + q
                gains[pl.ds(pl.multiple_of(group * 2 * bs, 2 * bs), 2 * bs), :] = data[d][
                    j, q, 3 * bs : 5 * bs, :
                ]
                third = data[d][j, q, 2 * bs : 3 * bs, :].astype(F32)
                third_turned = pltpu.roll(third, bs, 1)
                for i in range(2):
                    both = data[d][j, q, i * bs : (i + 1) * bs, :].astype(F32)
                    both_turned = pltpu.roll(both, bs, 1)
                    lefts = (both, both_turned, third if i == 0 else third_turned)
                    rights = (both_turned, both, third_turned if i == 0 else third)
                    where = [cols[d][here, (2 * q + i) * 3 + e] for e in range(3)]
                    row = pl.multiple_of(group * 2 * bs + i * bs, bs)
                    for tile in range(parts * pairs):
                        value_l = jnp.zeros((bs, 2 * bs), F32)
                        value_r = jnp.zeros((bs, 2 * bs), F32)
                        for e in range(3):
                            value_l = jnp.where(where[e] == 2 * tile, lefts[e], value_l)
                            value_r = jnp.where(where[e] == 2 * tile + 1, rights[e], value_r)
                        dyn[pl.ds(row, bs), tile * 2 * bs : (tile + 1) * 2 * bs] = jnp.where(
                            left, value_l, value_r
                        ).astype(BF)
        operator = op_ref[k].astype(F32)
        diagonal = jnp.concatenate(
            [jnp.where(left, operator, 0.0), jnp.where(left, 0.0, operator)], axis=0
        ).astype(BF)
        picks = []
        for o in range(2):
            block = blocks_ref[k, o]
            chosen[o * bs : (o + 1) * bs, :] = dyn[pl.ds(pl.multiple_of(block * bs, bs), bs), :]
            row = source[block // 2, pl.ds(here, 1), :]
            turned = pltpu.roll(row, bs, 1)
            picks.append(jnp.where(block % 2 == o, row, turned))
        image = tn(diagonal, chosen[...])
        masked = jnp.where(slot < counts_ref[k], image, 0.0).astype(BF)
        pick = jnp.where(lane_row < bs, picks[0], picks[1])
        source_image = fold(nn(split3(pick), diagonal)).astype(BF).astype(F32)
        innovation = jnp.where(
            lane_row < counts_ref[k], values_ref[pl.ds(k, 1), :] - source_image, 0.0
        )
        shift = fold(nt(split3(innovation), gains[...]))
        shift = shift + jnp.concatenate(
            [source[g, pl.ds(here, 1), :] for g in range(parts * pairs)], axis=1
        )
        offsets[j] = jnp.broadcast_to(shift, (8, ns))
        for g in range(parts * pairs):
            rows = slice(g * 2 * bs, (g + 1) * 2 * bs)
            elements[j, rows, :] = (
                dyn[rows, :].astype(F32) - nn(gains[rows, :], masked)
            ).astype(BF)
    if first == 0:
        begin = jnp.logical_and(s == 0, tm_ref[0] == 0)
        vec = jnp.where(begin, prior_ref[...], 0.0)
    else:
        vec = vec_in[0:1, :]
    step_rows = 256 if ns % 256 == 0 else ns
    for j in range(count):
        element = elements[j]
        vec = fold(nt(split3(vec), element)) + offsets[j, 0:1, :]
        for r in range(0, ns, step_rows):
            rows = slice(r, r + step_rows)
            if first == 0 and j == 0:
                across = lax.broadcasted_iota(jnp.int32, (step_rows, ns), 1)
                down = lax.broadcasted_iota(jnp.int32, (step_rows, ns), 0) + r
                unit = jnp.where(across == down, 1.0, 0.0).astype(BF)
                hi_ref[rows, :] = nt(unit, element).astype(BF)
                lo_ref[rows, :] = jnp.zeros((step_rows, ns), BF)
                continue
            if j == 0:
                hi, lo = hi_in[rows, :], lo_in[rows, :]
            else:
                hi, lo = hi_ref[rows, :], lo_ref[rows, :]
            if first == 0 and j == 1:
                moved = nt(hi, element)
            else:
                moved = nt(hi, element) + nt(lo, element)
            top = moved.astype(BF)
            hi_ref[rows, :] = top
            lo_ref[rows, :] = (moved - top.astype(F32)).astype(BF)
    vec_ref[...] = jnp.broadcast_to(vec, (8, ns))


def chunk_piece(
    position, span, cols, blocks, counts, data, small, obs_op, obs_values, prior, state, first, count
):
    parts = len(data)
    pairs, height, width = data[0].shape[1:]
    bs = width // 2
    ns = parts * pairs * width
    chunk = small[0].shape[0]
    if state is None:
        state = (jnp.zeros((8, 128), BF), jnp.zeros((8, 128), BF), jnp.zeros((8, 128), F32))
    return pl.pallas_call(
        functools.partial(chunk_kernel, parts, pairs, bs, chunk, first, count),
        grid_spec=pltpu.PrefetchScalarGridSpec(
            num_scalar_prefetch=4 + parts,
            grid=(),
            in_specs=vmem(2 * parts + 6),
            out_specs=vmem(5),
            scratch_shapes=[
                pltpu.VMEM((ns, ns), BF),
                pltpu.VMEM((ns, width), BF),
                pltpu.VMEM((parts * pairs, chunk, width), F32),
                pltpu.VMEM((width, ns), BF),
            ],
        ),
        out_shape=[
            jax.ShapeDtypeStruct((count, ns, ns), BF),
            jax.ShapeDtypeStruct((count, 8, ns), F32),
            jax.ShapeDtypeStruct((ns, ns), BF),
            jax.ShapeDtypeStruct((ns, ns), BF),
            jax.ShapeDtypeStruct((8, ns), F32),
        ],
        compiler_params=pltpu.CompilerParams(vmem_limit_bytes=VMEM_LIMIT),
        name=f"chunk_{first}",
    )(position, span, blocks, counts, *cols, *data, *small, obs_op, obs_values, prior, *state)


def apply_map(row, hi, lo):
    parts = split3(row)
    return fold(nn(parts, hi) + nn(parts, lo))


def join_maps(one, two, hi_ref, lo_ref, vec_ref):
    ns = hi_ref.shape[0]
    step = 256 if ns % 256 == 0 else ns
    for r in range(0, ns, step):
        rows = slice(r, r + step)
        product = nn(one[0][rows, :], two[0][...]) + (
            nn(one[0][rows, :], two[1][...]) + nn(one[1][rows, :], two[0][...])
        )
        top = product.astype(BF)
        hi_ref[rows, :] = top
        lo_ref[rows, :] = (product - top.astype(F32)).astype(BF)
    vec = apply_map(one[2][0:1, :], two[0][...], two[1][...]) + two[2][0:1, :]
    vec_ref[...] = jnp.broadcast_to(vec, vec_ref.shape)


def pair_kernel(bit, s_ref, *refs):
    own, other, out = refs[:3], refs[3:6], refs[6:9]
    halves = refs[9:11]
    earlier = (s_ref[0] & bit) == 0

    @pl.when(earlier)
    def _():
        join_maps(own, other, *out)

    @pl.when(jnp.logical_not(earlier))
    def _():
        join_maps(other, own, *out)

    half = out[0].shape[0] // 2
    start = pl.multiple_of((s_ref[0] & 1) * half, half)
    halves[0][...] = out[0][pl.ds(start, half), :]
    halves[1][...] = out[1][pl.ds(start, half), :]


def join_pair(position, own, other, bit):
    ns = own[0].shape[0]
    return pl.pallas_call(
        functools.partial(pair_kernel, bit),
        grid_spec=pltpu.PrefetchScalarGridSpec(
            num_scalar_prefetch=1, grid=(), in_specs=vmem(6), out_specs=vmem(5)
        ),
        out_shape=[
            jax.ShapeDtypeStruct((ns, ns), BF),
            jax.ShapeDtypeStruct((ns, ns), BF),
            jax.ShapeDtypeStruct((8, ns), F32),
            jax.ShapeDtypeStruct((ns // 2, ns), BF),
            jax.ShapeDtypeStruct((ns // 2, ns), BF),
        ],
        compiler_params=pltpu.CompilerParams(vmem_limit_bytes=VMEM_LIMIT),
        name=f"join_{bit}",
    )(position, *own, *other)


def wide_kernel(bit, s_ref, *refs):
    own, near, far, vec_other = refs[:3], refs[3:5], refs[5:7], refs[7]
    out, other = refs[8:11], refs[11:13]
    half = own[0].shape[0] // 2
    start = pl.multiple_of((s_ref[0] & 1) * half, half)
    rest = pl.multiple_of(half - (s_ref[0] & 1) * half, half)
    for i in range(2):
        other[i][pl.ds(start, half), :] = near[i][...]
        other[i][pl.ds(rest, half), :] = far[i][...]
    earlier = (s_ref[0] & bit) == 0

    @pl.when(earlier)
    def _():
        join_maps(own, (other[0], other[1], vec_other), *out)

    @pl.when(jnp.logical_not(earlier))
    def _():
        join_maps((other[0], other[1], vec_other), own, *out)


def join_wide(position, own, near, far, vec_other, bit):
    ns = own[0].shape[0]
    whole = jax.ShapeDtypeStruct((ns, ns), BF)
    return pl.pallas_call(
        functools.partial(wide_kernel, bit),
        grid_spec=pltpu.PrefetchScalarGridSpec(
            num_scalar_prefetch=1, grid=(), in_specs=vmem(8), out_specs=vmem(5)
        ),
        out_shape=[whole, whole, jax.ShapeDtypeStruct((8, ns), F32), whole, whole],
        compiler_params=pltpu.CompilerParams(vmem_limit_bytes=VMEM_LIMIT),
        name=f"join_{bit}",
    )(position, *own, *near, *far, vec_other)


def hop_kernel(row_ref, hi_ref, lo_ref, vec_ref, out_ref):
    out_ref[...] = apply_map(row_ref[...], hi_ref[...], lo_ref[...]) + vec_ref[0:1, :]


def hop(row, hi, lo, vec):
    return pl.pallas_call(
        hop_kernel,
        in_specs=vmem(4),
        out_specs=vmem(1)[0],
        out_shape=jax.ShapeDtypeStruct(row.shape, F32),
        compiler_params=pltpu.CompilerParams(vmem_limit_bytes=VMEM_LIMIT),
        name="hop",
    )(row, hi, lo, vec)


def sweep_kernel(levels, pieces, parts, s_ref, tm_ref, *refs):
    row_ref, prior_ref = refs[:2]
    maps = [refs[2 + 3 * n : 5 + 3 * n] for n in range(levels)]
    refs = refs[2 + 3 * levels :]
    elements, offsets = refs[:pieces], refs[pieces : 2 * pieces]
    outs = refs[2 * pieces : 2 * pieces + parts]
    current_ref, spread = refs[2 * pieces + parts :]
    s = s_ref[0]
    begin = jnp.logical_and(s == 0, tm_ref[0] == 0)
    current_ref[...] = row_ref[...] + jnp.where(begin, prior_ref[...], 0.0)
    for n in reversed(range(levels)):
        hi, lo, vec = maps[n]

        @pl.when((s & (1 << n)) != 0)
        def _():
            current_ref[...] = apply_map(current_ref[...], hi[...], lo[...]) + vec[0:1, :]

    current = current_ref[...]
    at = 0
    width = spread.shape[2]
    for p in range(pieces):
        for j in range(elements[p].shape[0]):
            current = fold(nt(split3(current), elements[p][j])) + offsets[p][j, 0:1, :]
            for d in range(parts):
                spread[d, at : at + 1, :] = current[:, d * width : (d + 1) * width]
            at += 1
    for d in range(parts):
        outs[d][...] = spread[s ^ d]


def sweep(position, span, row, prior, maps, elements, offsets, parts):
    ns = row.shape[1]
    levels, pieces = len(maps), len(elements)
    chunk = sum(e.shape[0] for e in elements)
    width = ns // parts
    return pl.pallas_call(
        functools.partial(sweep_kernel, levels, pieces, parts),
        grid_spec=pltpu.PrefetchScalarGridSpec(
            num_scalar_prefetch=2,
            grid=(),
            in_specs=vmem(2 + 3 * levels + 2 * pieces),
            out_specs=vmem(parts),
            scratch_shapes=[
                pltpu.VMEM((1, ns), F32),
                pltpu.VMEM((parts, chunk, width), F32),
            ],
        ),
        out_shape=[jax.ShapeDtypeStruct((chunk, width), F32)] * parts,
        compiler_params=pltpu.CompilerParams(vmem_limit_bytes=VMEM_LIMIT),
        name="sweep",
    )(position, span, row, prior, *[m for trio in maps for m in trio], *elements, *offsets)


def body(dyn_cols, dyn_vals, obs_blocks, obs_op, obs_counts, obs_values, gain, sources, prior):
    steps, lb, bs, width = dyn_vals.shape
    parts = lax.axis_size("state")
    spans = lax.axis_size("tm")
    chunk = steps // parts
    ns = prior.shape[0]
    s = lax.axis_index("state")
    t = lax.axis_index("tm")
    position = s.reshape(1).astype(jnp.int32)
    span = t.reshape(1).astype(jnp.int32)
    prior_row = prior.reshape(1, ns)

    def across(x, d):
        return lax.ppermute(x, "state", [(i, i ^ d) for i in range(parts)])

    order = sorted(range(1, parts), reverse=True)
    table = jnp.concatenate(
        [sources, dyn_cols.reshape(steps, -1).astype(F32)], axis=1
    ).reshape(parts, chunk, -1)
    small = [lax.dynamic_index_in_dim(table, s ^ d, 0, False) for d in range(parts)]
    small = [small[0]] + [across(small[d], d) for d in range(1, parts)]
    cols = [x[:, lb * bs :].astype(jnp.int32) for x in small]
    small = [x[:, : lb * bs] for x in small]

    per = 2 if chunk % 2 == 0 else 1
    state = None
    elements, offsets = [], []
    for first in range(0, chunk, per):
        packed = pack(position, dyn_vals, gain, parts, chunk, first, per)
        arrived = {d: across(packed[d], d) for d in order}
        data = [packed[0]] + [arrived[d] for d in range(1, parts)]
        element, offset, *state = chunk_piece(
            position, span, cols, obs_blocks, obs_counts, data, small, obs_op, obs_values,
            prior_row, state, first, per,
        )
        elements.append(element)
        offsets.append(offset)

    maps = []
    bit = 1
    while bit < parts:
        if bit == 1:
            other = [across(x, bit) for x in state]
            maps.append(other)
            *state, half_hi, half_lo = join_pair(position, state, other, bit)
        else:
            near = [across(half_hi, bit), across(half_lo, bit)]
            vec_other = across(state[2], bit)
            far = [across(x, 1) for x in near]
            *state, other_hi, other_lo = join_wide(position, state, near, far, vec_other, bit)
            maps.append([other_hi, other_lo, vec_other])
        bit *= 2

    current = state[2][0:1, :]
    entry = jnp.zeros((1, ns), F32)
    for h in range(spans - 1):
        arriving = lax.ppermute(current, "tm", [(h, h + 1)])
        entry = entry + arriving
        current = hop(arriving, *state)

    mine = sweep(position, span, entry, prior_row, maps, elements, offsets, parts)
    got = [mine[0]] + [across(mine[d], d) for d in range(1, parts)]
    bit = 1
    while bit < parts:
        swapped = [got[d ^ bit] for d in range(parts)]
        got = [jnp.where((s & bit) != 0, b, a) for a, b in zip(got, swapped)]
        bit *= 2
    return jnp.concatenate(got, axis=0)


def solution(mesh):
    return jax.shard_map(
        body,
        mesh=mesh,
        in_specs=(
            P("tm", "state", None),
            P("tm", "state", None, None),
            P("tm", None),
            P("tm", None, None),
            P("tm"),
            P("tm", None),
            P("tm", "state", None),
            P("tm", "state"),
            P(),
        ),
        out_specs=P("tm", "state"),
        check_vma=False,
    )
```

```python
import functools

import jax
import jax.numpy as jnp
from jax import lax
from jax.experimental import pallas as pl
from jax.experimental.pallas import tpu as pltpu
from jax.sharding import PartitionSpec as P


BF = jnp.bfloat16
F32 = jnp.float32
VMEM_LIMIT = 8 * 1024 * 1024
ROWS = 16


def nt(a, b):
    return lax.dot_general(a, b, (((1,), (1,)), ((), ())), preferred_element_type=F32)


def nn(a, b):
    return lax.dot_general(a, b, (((1,), (0,)), ((), ())), preferred_element_type=F32)


def tn(a, b):
    return lax.dot_general(a, b, (((0,), (0,)), ((), ())), preferred_element_type=F32)


def split3(row):
    hi = row.astype(BF).astype(F32)
    rest = row - hi
    mid = rest.astype(BF).astype(F32)
    low = rest - mid
    at = lax.broadcasted_iota(jnp.int32, (ROWS, row.shape[1]), 0)
    zero = jnp.zeros((), F32)
    return jnp.where(at == 0, hi, jnp.where(at == 1, mid, jnp.where(at == 2, low, zero))).astype(BF)


def turn(block, by):
    return jnp.concatenate([block[:, by:], block[:, :by]], axis=1)


def fold(rows):
    return jnp.sum(rows, axis=0, keepdims=True)


def vmem(n):
    return [pl.BlockSpec(memory_space=pltpu.VMEM)] * n


def pack_kernel(parts, pairs, bs, chunk, table, s_ref, tm_ref, *refs):
    vals, gains = refs[:parts], refs[parts : 2 * parts]
    refs = refs[2 * parts :]
    if table:
        source_ref, cols_ref = refs[:2]
        refs = refs[2:]
        tables = refs[parts:]
        for d in range(parts):
            tables[d][...] = jnp.zeros(tables[d].shape, F32)
            begin = pl.multiple_of((s_ref[0] ^ d) * chunk, chunk)
            tables[d][:chunk, :] = source_ref[pl.ds(begin, chunk), :]
            for e in range(cols_ref.shape[0]):
                for i in range(cols_ref.shape[1]):
                    at = chunk + e * cols_ref.shape[1] + i
                    line = cols_ref[e, i : i + 1, :].astype(F32)
                    tables[d][at : at + 1, : line.shape[1]] = line
    outs = refs[:parts]
    for d in range(parts):
        for q in range(pairs):
            for i in range(2):
                outs[d][0, q, i * bs : (i + 1) * bs, :] = vals[d][0, 2 * q + i, :, : 2 * bs]
            base = 2 * bs
            third = jnp.concatenate(
                [vals[d][0, 2 * q, :, 2 * bs :], vals[d][0, 2 * q + 1, :, 2 * bs :]], axis=1
            )
            outs[d][0, q, base : base + bs, :] = third
            base = 3 * bs
            outs[d][0, q, base : base + 2 * bs, :] = gains[d][0, q * 2 * bs : (q + 1) * 2 * bs, :]


def pack(position, span, dyn_vals, gain, parts, chunk, first, count, table=()):
    _, lb, bs, width = dyn_vals.shape
    rows, obs = gain.shape[1:]
    pairs = lb // 2

    def from_part(d, trail):
        return lambda j, s, t: ((s[0] ^ d) * chunk + first + j,) + (0,) * trail

    shape = (count, pairs, 5 * bs, 2 * bs)
    tables = [jax.ShapeDtypeStruct((chunk + 3 * lb, lb * bs), F32)] * (parts if table else 0)
    return pl.pallas_call(
        functools.partial(pack_kernel, parts, pairs, bs, chunk, bool(table)),
        grid_spec=pltpu.PrefetchScalarGridSpec(
            num_scalar_prefetch=2,
            grid=(count,),
            in_specs=[pl.BlockSpec((1, lb, bs, width), from_part(d, 3)) for d in range(parts)]
            + [pl.BlockSpec((1, rows, obs), from_part(d, 2)) for d in range(parts)]
            + vmem(len(table)),
            out_specs=[pl.BlockSpec((1,) + shape[1:], lambda j, s, t: (j, 0, 0, 0))] * parts
            + vmem(len(tables)),
        ),
        out_shape=[jax.ShapeDtypeStruct(shape, BF)] * parts + tables,
        compiler_params=pltpu.CompilerParams(vmem_limit_bytes=VMEM_LIMIT),
    )(position, span, *([dyn_vals] * parts), *([gain] * parts), *table)


def chunk_kernel(
    parts, pairs, bs, chunk, first, count, s_ref, tm_ref, blocks_ref, counts_ref, *refs
):
    cols, refs = refs[:parts], refs[parts:]
    data, small = refs[:parts], refs[parts : 2 * parts]
    op_ref, values_ref, prior_ref, hi_in, lo_in, vec_in = refs[2 * parts : 2 * parts + 6]
    elements, offsets, hi_ref, lo_ref, vec_ref = refs[2 * parts + 6 : 2 * parts + 11]
    dyn, gains, source, chosen = refs[2 * parts + 11 :]
    s = s_ref[0]
    ns = parts * pairs * 2 * bs
    lane = lax.broadcasted_iota(jnp.int32, (bs, 2 * bs), 1)
    left = lane < bs
    zero = jnp.zeros((), BF)
    tiles = parts * pairs
    lane_row = lax.broadcasted_iota(jnp.int32, (1, 2 * bs), 1)
    slot = lax.broadcasted_iota(jnp.int32, (2 * bs, 1), 0)
    for d in range(parts):
        for q in range(pairs):
            source[(s ^ d) * pairs + q] = small[d][:chunk, q * 2 * bs : (q + 1) * 2 * bs]
    for j in range(count):
        here = first + j
        k = s * chunk + here
        dyn[...] = jnp.zeros(dyn.shape, BF)
        for d in range(parts):
            for q in range(pairs):
                group = (s ^ d) * pairs + q
                gains[pl.ds(pl.multiple_of(group * 2 * bs, 2 * bs), 2 * bs), :] = data[d][
                    j, q, 3 * bs : 5 * bs, :
                ]
                third = data[d][j, q, 2 * bs : 3 * bs, :]
                third_turned = turn(third, bs)
                for i in range(2):
                    both = data[d][j, q, i * bs : (i + 1) * bs, :]
                    both_turned = turn(both, bs)
                    lefts = (both, both_turned, third if i == 0 else third_turned)
                    rights = (both_turned, both, third_turned if i == 0 else third)
                    row = pl.multiple_of(group * 2 * bs + i * bs, bs)
                    for e in range(3):
                        column = cols[d][chunk + e * 2 * pairs + 2 * q + i, k].astype(jnp.int32)
                        side = column % 2
                        value = jnp.where(
                            side == 0,
                            jnp.where(left, lefts[e], zero),
                            jnp.where(left, zero, rights[e]),
                        )
                        dyn[side * tiles + column // 2, pl.ds(row, bs), :] = value
        operator = op_ref[k].astype(F32)
        diagonal = jnp.concatenate(
            [jnp.where(left, operator, 0.0), jnp.where(left, 0.0, operator)], axis=0
        ).astype(BF)
        picks = []
        for o in range(2):
            block = blocks_ref[o, k]
            for tile in range(tiles):
                found = pl.ds(pl.multiple_of(block * bs, bs), bs)
                chosen[o * bs : (o + 1) * bs, tile * 2 * bs : (tile + 1) * 2 * bs] = (
                    dyn[tile, found, :] + dyn[tiles + tile, found, :]
                )
            row = source[block // 2, pl.ds(here, 1), :]
            turned = pltpu.roll(row, bs, 1)
            picks.append(jnp.where(block % 2 == o, row, turned))
        image = tn(diagonal, chosen[...])
        masked = jnp.where(slot < counts_ref[k], image, 0.0).astype(BF)
        pick = jnp.where(lane_row < bs, picks[0], picks[1])
        source_image = fold(nn(split3(pick), diagonal)).astype(BF).astype(F32)
        innovation = jnp.where(
            lane_row < counts_ref[k], values_ref[pl.ds(k, 1), :] - source_image, 0.0
        )
        shift = fold(nt(split3(innovation), gains[...]))
        shift = shift + jnp.concatenate(
            [source[g, pl.ds(here, 1), :] for g in range(parts * pairs)], axis=1
        )
        offsets[j] = jnp.broadcast_to(shift, (8, ns))
        for g in range(parts * pairs):
            rows = slice(g * 2 * bs, (g + 1) * 2 * bs)
            correction = nn(gains[rows, :], masked)
            for tile in range(tiles):
                lanes = slice(tile * 2 * bs, (tile + 1) * 2 * bs)
                forward = (dyn[tile, rows, :] + dyn[tiles + tile, rows, :]).astype(F32)
                elements[j, rows, lanes] = (forward - correction[:, lanes]).astype(BF)
    if first == 0:
        begin = jnp.logical_and(s == 0, tm_ref[0] == 0)
        vec = jnp.where(begin, prior_ref[...], 0.0)
    else:
        vec = vec_in[...]
    step_rows = 256 if ns % 256 == 0 else ns
    for j in range(count):
        element = elements[j]
        vec = fold(nt(split3(vec), element)) + offsets[j, 0:1, :]
        for r in range(0, ns, step_rows):
            rows = slice(r, r + step_rows)
            if first == 0 and j == 0:
                across = lax.broadcasted_iota(jnp.int32, (step_rows, ns), 1)
                down = lax.broadcasted_iota(jnp.int32, (step_rows, ns), 0) + r
                unit = jnp.where(across == down, 1.0, 0.0).astype(BF)
                hi_ref[rows, :] = nt(unit, element).astype(BF)
                lo_ref[rows, :] = jnp.zeros((step_rows, ns), BF)
                continue
            if j == 0:
                hi, lo = hi_in[rows, :], lo_in[rows, :]
            else:
                hi, lo = hi_ref[rows, :], lo_ref[rows, :]
            if first == 0 and j == 1:
                moved = nt(hi, element)
            else:
                moved = nt(hi, element) + nt(lo, element)
            top = moved.astype(BF)
            hi_ref[rows, :] = top
            lo_ref[rows, :] = (moved - top.astype(F32)).astype(BF)
    vec_ref[...] = vec


def chunk_piece(
    position, span, blocks, counts, data, small, obs_op, obs_values, prior, state, chunk, first, count
):
    parts = len(data)
    pairs, _, width = data[0].shape[1:]
    bs = width // 2
    ns = parts * pairs * width
    if state is None:
        state = (data[0], data[0], prior)
    return pl.pallas_call(
        functools.partial(chunk_kernel, parts, pairs, bs, chunk, first, count),
        grid_spec=pltpu.PrefetchScalarGridSpec(
            num_scalar_prefetch=4,
            grid=(),
            in_specs=[pl.BlockSpec(memory_space=pltpu.SMEM)] * parts + vmem(2 * parts + 6),
            out_specs=vmem(5),
            scratch_shapes=[
                pltpu.VMEM((2 * parts * pairs, ns, width), BF),
                pltpu.VMEM((ns, width), BF),
                pltpu.VMEM((parts * pairs, chunk, width), F32),
                pltpu.VMEM((width, ns), BF),
            ],
        ),
        out_shape=[
            jax.ShapeDtypeStruct((count, ns, ns), BF),
            jax.ShapeDtypeStruct((count, 8, ns), F32),
            jax.ShapeDtypeStruct((ns, ns), BF),
            jax.ShapeDtypeStruct((ns, ns), BF),
            jax.ShapeDtypeStruct((1, ns), F32),
        ],
        compiler_params=pltpu.CompilerParams(vmem_limit_bytes=VMEM_LIMIT),
    )(
        position, span, blocks, counts, *small, *data, *small, obs_op, obs_values, prior, *state,
    )


def apply_map(row, hi, lo):
    parts = split3(row)
    return fold(nn(parts, hi) + nn(parts, lo))


def join_kernel(hi_one, lo_one, hi_two, lo_two, hi_ref, lo_ref):
    ns = hi_ref.shape[0]
    step = 256 if ns % 256 == 0 else ns
    for r in range(0, ns, step):
        rows = slice(r, r + step)
        product = nn(hi_one[rows, :], hi_two[...]) + (
            nn(hi_one[rows, :], lo_two[...]) + nn(lo_one[rows, :], hi_two[...])
        )
        top = product.astype(BF)
        hi_ref[rows, :] = top
        lo_ref[rows, :] = (product - top.astype(F32)).astype(BF)


def join(one, two):
    return pl.pallas_call(
        join_kernel,
        in_specs=vmem(4),
        out_specs=vmem(2),
        out_shape=[jax.ShapeDtypeStruct(x.shape, BF) for x in two],
        compiler_params=pltpu.CompilerParams(vmem_limit_bytes=VMEM_LIMIT),
        name="join",
    )(*one, *two)


def hop_kernel(row_ref, hi_ref, lo_ref, vec_ref, out_ref):
    out_ref[...] = apply_map(row_ref[...], hi_ref[...], lo_ref[...]) + vec_ref[...]


def hop(row, hi, lo, vec):
    return pl.pallas_call(
        hop_kernel,
        in_specs=vmem(4),
        out_specs=vmem(1)[0],
        out_shape=jax.ShapeDtypeStruct(row.shape, F32),
        compiler_params=pltpu.CompilerParams(vmem_limit_bytes=VMEM_LIMIT),
        name="hop",
    )(row, hi, lo, vec)


def span_kernel(leaders, whole, early, s_ref, tm_ref, row_ref, direct_ref, *refs):
    maps, out_ref = [refs[3 * n : 3 * n + 3] for n in range(leaders)], refs[3 * leaders]
    for mine in range(leaders):

        @pl.when(s_ref[0] // 2 == mine)
        def _():
            current = row_ref[...]
            for p in range(leaders if whole else mine):
                hi, lo, vec = maps[p ^ mine]
                current = apply_map(current, hi[...], lo[...]) + vec[...]
            if not whole:
                current = jnp.where(tm_ref[0] < early, direct_ref[...], current)
            out_ref[...] = current


def span_hop(position, span, row, direct, maps, whole, early):
    leaders = len(maps)
    return pl.pallas_call(
        functools.partial(span_kernel, leaders, whole, early),
        grid_spec=pltpu.PrefetchScalarGridSpec(
            num_scalar_prefetch=2,
            grid=(),
            in_specs=vmem(2 + 3 * leaders),
            out_specs=vmem(1)[0],
        ),
        out_shape=jax.ShapeDtypeStruct(row.shape, F32),
        compiler_params=pltpu.CompilerParams(vmem_limit_bytes=VMEM_LIMIT),
        name="span_hop" if whole else "lead",
    )(position, span, row, direct, *[m for trio in maps for m in trio])


def sweep_kernel(pieces, parts, s_ref, tm_ref, *refs):
    own_ref, told_ref, prior_ref, hi, lo, vec = refs[:6]
    refs = refs[6:]
    elements, offsets = refs[:pieces], refs[pieces : 2 * pieces]
    outs = refs[2 * pieces : 2 * pieces + parts]
    current_ref, spread = refs[2 * pieces + parts :]
    s = s_ref[0]
    begin = jnp.logical_and(s == 0, tm_ref[0] == 0)

    @pl.when(s % 2 == 0)
    def _():
        current_ref[...] = told_ref[...] + jnp.where(begin, prior_ref[...], 0.0)

    @pl.when(s % 2 == 1)
    def _():
        current_ref[...] = apply_map(own_ref[...], hi[...], lo[...]) + vec[...]

    current = current_ref[...]
    at = 0
    width = spread.shape[2]
    for p in range(pieces):
        for j in range(elements[p].shape[0]):
            current = fold(nt(split3(current), elements[p][j])) + offsets[p][j, 0:1, :]
            for d in range(parts):
                spread[d, at : at + 1, :] = current[:, d * width : (d + 1) * width]
            at += 1
    for d in range(parts):
        outs[d][...] = spread[s ^ d]


def sweep(position, span, own, told, prior, even, elements, offsets, parts):
    ns = own.shape[1]
    pieces = len(elements)
    chunk = sum(e.shape[0] for e in elements)
    width = ns // parts
    return pl.pallas_call(
        functools.partial(sweep_kernel, pieces, parts),
        grid_spec=pltpu.PrefetchScalarGridSpec(
            num_scalar_prefetch=2,
            grid=(),
            in_specs=vmem(6 + 2 * pieces),
            out_specs=vmem(parts),
            scratch_shapes=[
                pltpu.VMEM((1, ns), F32),
                pltpu.VMEM((parts, chunk, width), F32),
            ],
        ),
        out_shape=[jax.ShapeDtypeStruct((chunk, width), F32)] * parts,
        compiler_params=pltpu.CompilerParams(vmem_limit_bytes=VMEM_LIMIT),
        name="sweep",
    )(position, span, own, told, prior, *even, *elements, *offsets)


PIECES = 4


def piece_sizes(chunk):
    base, more = divmod(chunk, PIECES)
    return [base + 1] * more + [base] * (PIECES - more)


def means(dyn_cols, dyn_vals, obs_blocks, obs_op, obs_counts, obs_values, gain, sources, prior):
    steps, _, _, _ = dyn_vals.shape
    parts = lax.axis_size("state")
    spans = lax.axis_size("tm")
    chunk = steps // parts
    ns = prior.shape[0]
    s = lax.axis_index("state")
    t = lax.axis_index("tm")
    position = s.reshape(1).astype(jnp.int32)
    span = t.reshape(1).astype(jnp.int32)
    prior_row = prior.reshape(1, ns)

    def across(x, d):
        return lax.ppermute(x, "state", [(i, i ^ d) for i in range(parts)])

    def send(x, pairs):
        return lax.ppermute(x, ("tm", "state"), [(a * parts + b, c * parts + e) for (a, b), (c, e) in pairs])

    order = sorted(range(1, parts), reverse=True)
    sizes = piece_sizes(chunk)
    firsts = [sum(sizes[:n]) for n in range(len(sizes))]
    vals_far = pltpu.with_memory_space_constraint(dyn_vals, pltpu.HBM)
    gain_far = pltpu.with_memory_space_constraint(gain, pltpu.HBM)
    pieces = []
    for n, (first, size) in enumerate(zip(firsts, sizes)):
        source_arrays = (vals_far, gain_far) if n == 0 else (dyn_vals, gain)
        table = (sources, dyn_cols.transpose(2, 1, 0)) if n == 0 else ()
        packed = pack(position, span, *source_arrays, parts, chunk, first, size, table)
        arrived = {0: packed[0]}
        for d in order:
            arrived[d] = across(packed[d], d)
        pieces.append([arrived[d] for d in range(parts)])
        if n == 0:
            small = {0: packed[parts]}
            for d in order:
                small[d] = across(packed[parts + d], d)
            small = [small[d] for d in range(parts)]

    state = None
    elements, offsets = [], []
    for first, size, data in zip(firsts, sizes, pieces):
        element, offset, *state = chunk_piece(
            position, span, obs_blocks.T, obs_counts, data, small, obs_op, obs_values,
            prior_row, state, chunk, first, size,
        )
        elements.append(element)
        offsets.append(offset)
    hi, lo, vec = state

    leads = [2 * p + 1 for p in range(parts // 2)]
    to_lead = [((a, l - 1), (a, l)) for a in range(spans) for l in leads]
    vec_even = send(vec, to_lead)
    hi_even = send(hi, to_lead)
    lo_even = send(lo, to_lead)
    pair_vec = hop(vec_even, hi, lo, vec)
    pair_hi, pair_lo = join((hi_even, lo_even), (hi, lo))
    pair = (pair_hi, pair_lo, pair_vec)

    early = min(2, spans - 1)
    maps = [pair]
    for d in range(2, parts, 2):
        pairs = [((a, l), (a, l ^ d)) for a in range(early, spans) for l in leads]
        far = []
        for x in pair:
            far.append(send(x, pairs))
        maps.append(tuple(far))

    direct = jnp.zeros((1, ns), F32)
    entry = jnp.zeros((1, ns), F32)
    current = pair_vec
    for g in range(early):
        for p in range(1, len(leads)):
            arriving = send(current, [((g, leads[p - 1]), (g, leads[p]))])
            direct = direct + arriving
            current = hop(arriving, *pair)
        if g + 1 < early:
            arriving = send(current, [((g, leads[-1]), (g + 1, leads[0]))])
            direct = direct + arriving
            current = hop(arriving, *pair)
        else:
            for l in leads:
                entry = entry + send(current, [((g, leads[-1]), (g + 1, l))])

    arriving = entry
    for h in range(early, spans - 1):
        current = span_hop(position, span, arriving, direct, maps, True, early)
        arriving = send(current, [((h, l), (h + 1, l)) for l in leads])
        entry = entry + arriving

    own = span_hop(position, span, entry, direct, maps, False, early)
    told = send(own, [(b, a) for a, b in to_lead])
    mine = sweep(
        position, span, own, told, prior_row, (hi_even, lo_even, vec_even), elements, offsets, parts
    )
    got = [mine[0]] + [across(mine[d], d) for d in range(1, parts)]
    bit = 1
    while bit < parts:
        swapped = [got[d ^ bit] for d in range(parts)]
        got = [jnp.where((s & bit) != 0, b, a) for a, b in zip(got, swapped)]
        bit *= 2
    return jnp.concatenate(got, axis=0)


def solution(mesh):
    return jax.shard_map(
        means,
        mesh=mesh,
        in_specs=(
            P("tm", "state", None),
            P("tm", "state", None, None),
            P("tm", None),
            P("tm", None, None),
            P("tm"),
            P("tm", None),
            P("tm", "state", None),
            P("tm", "state"),
            P(),
        ),
        out_specs=P("tm", "state"),
        check_vma=False,
    )
```

```python
import functools

import jax
import jax.numpy as jnp
from jax import lax
from jax.experimental import pallas as pl
from jax.experimental.pallas import tpu as pltpu
from jax.sharding import PartitionSpec as P


BF = jnp.bfloat16
F32 = jnp.float32
VMEM_LIMIT = 12 * 1024 * 1024
ROWS = 16


def nt(a, b):
    return lax.dot_general(a, b, (((1,), (1,)), ((), ())), preferred_element_type=F32)


def nn(a, b):
    return lax.dot_general(a, b, (((1,), (0,)), ((), ())), preferred_element_type=F32)


def tn(a, b):
    return lax.dot_general(a, b, (((0,), (0,)), ((), ())), preferred_element_type=F32)


def split3(row):
    hi = row.astype(BF).astype(F32)
    rest = row - hi
    mid = rest.astype(BF).astype(F32)
    low = rest - mid
    at = lax.broadcasted_iota(jnp.int32, (ROWS, row.shape[1]), 0)
    zero = jnp.zeros((), F32)
    return jnp.where(at == 0, hi, jnp.where(at == 1, mid, jnp.where(at == 2, low, zero))).astype(BF)


def step_of(ns):
    return 256 if ns % 256 == 0 else ns


def turn(block, by):
    return jnp.concatenate([block[:, by:], block[:, :by]], axis=1)


def fold(rows):
    return jnp.sum(rows, axis=0, keepdims=True)


def vmem(n):
    return [pl.BlockSpec(memory_space=pltpu.VMEM)] * n


def pack_kernel(parts, pairs, bs, chunk, table, s_ref, tm_ref, *refs):
    vals, gains = refs[:parts], refs[parts : 2 * parts]
    refs = refs[2 * parts :]
    if table:
        source_ref, cols_ref = refs[:2]
        refs = refs[2:]
        tables = refs[parts:]
        for d in range(parts):
            tables[d][...] = jnp.zeros(tables[d].shape, F32)
            begin = pl.multiple_of((s_ref[0] ^ d) * chunk, chunk)
            tables[d][:chunk, :] = source_ref[pl.ds(begin, chunk), :]
            for e in range(cols_ref.shape[0]):
                for i in range(cols_ref.shape[1]):
                    at = chunk + e * cols_ref.shape[1] + i
                    line = cols_ref[e, i : i + 1, :].astype(F32)
                    tables[d][at : at + 1, : line.shape[1]] = line
    outs = refs[:parts]
    for d in range(parts):
        for q in range(pairs):
            for i in range(2):
                outs[d][0, q, i * bs : (i + 1) * bs, :] = vals[d][0, 2 * q + i, :, : 2 * bs]
            base = 2 * bs
            third = jnp.concatenate(
                [vals[d][0, 2 * q, :, 2 * bs :], vals[d][0, 2 * q + 1, :, 2 * bs :]], axis=1
            )
            outs[d][0, q, base : base + bs, :] = third
            base = 3 * bs
            outs[d][0, q, base : base + 2 * bs, :] = gains[d][0, q * 2 * bs : (q + 1) * 2 * bs, :]


def pack(position, span, dyn_vals, gain, parts, chunk, first, count, table=()):
    _, lb, bs, width = dyn_vals.shape
    rows, obs = gain.shape[1:]
    pairs = lb // 2

    def from_part(d, trail):
        return lambda j, s, t: ((s[0] ^ d) * chunk + first + j,) + (0,) * trail

    shape = (count, pairs, 5 * bs, 2 * bs)
    tables = [jax.ShapeDtypeStruct((chunk + 3 * lb, lb * bs), F32)] * (parts if table else 0)
    return pl.pallas_call(
        functools.partial(pack_kernel, parts, pairs, bs, chunk, bool(table)),
        grid_spec=pltpu.PrefetchScalarGridSpec(
            num_scalar_prefetch=2,
            grid=(count,),
            in_specs=[pl.BlockSpec((1, lb, bs, width), from_part(d, 3)) for d in range(parts)]
            + [pl.BlockSpec((1, rows, obs), from_part(d, 2)) for d in range(parts)]
            + vmem(len(table)),
            out_specs=[pl.BlockSpec((1,) + shape[1:], lambda j, s, t: (j, 0, 0, 0))] * parts
            + vmem(len(tables)),
        ),
        out_shape=[jax.ShapeDtypeStruct(shape, BF)] * parts + tables,
        compiler_params=pltpu.CompilerParams(vmem_limit_bytes=VMEM_LIMIT),
    )(position, span, *([dyn_vals] * parts), *([gain] * parts), *table)


def plan_kernel(parts, chunk, *refs):
    small, blocks, counts, out_ref = refs[:parts], refs[parts], refs[parts + 1], refs[parts + 2]
    steps = counts.shape[1]
    each = small[0].shape[0] - chunk
    for d in range(parts):
        out_ref[d * each : (d + 1) * each, :] = small[d][chunk:, :steps].astype(jnp.int32)
    out_ref[parts * each : parts * each + 2, :] = blocks[...]
    out_ref[parts * each + 2 : parts * each + 3, :] = counts[...]


def plan_of(small, blocks, counts, chunk):
    parts = len(small)
    each = small[0].shape[0] - chunk
    return pl.pallas_call(
        functools.partial(plan_kernel, parts, chunk),
        in_specs=vmem(parts + 2),
        out_specs=vmem(1)[0],
        out_shape=jax.ShapeDtypeStruct((parts * each + 3, counts.shape[1]), jnp.int32),
        compiler_params=pltpu.CompilerParams(vmem_limit_bytes=VMEM_LIMIT),
        name="plan",
    )(*small, blocks, counts)


def chunk_kernel(
    parts, pairs, bs, chunk, first, count, s_ref, tm_ref, plan_ref, *refs
):
    each = 6 * pairs
    data, small = refs[:parts], refs[parts : 2 * parts]
    op_ref, values_ref, prior_ref, map_in, vec_in = refs[2 * parts : 2 * parts + 5]
    elements, offsets, map_ref, vec_ref = refs[2 * parts + 5 : 2 * parts + 9]
    dyn, gains, source, chosen = refs[2 * parts + 9 :]
    s = s_ref[0]
    ns = parts * pairs * 2 * bs
    lane = lax.broadcasted_iota(jnp.int32, (bs, 2 * bs), 1)
    left = lane < bs
    zero = jnp.zeros((), BF)
    tiles = parts * pairs
    lane_row = lax.broadcasted_iota(jnp.int32, (1, 2 * bs), 1)
    slot = lax.broadcasted_iota(jnp.int32, (2 * bs, 1), 0)
    for d in range(parts):
        for q in range(pairs):
            source[(s ^ d) * pairs + q] = small[d][:chunk, q * 2 * bs : (q + 1) * 2 * bs]
    for j in range(count):
        here = first + j
        k = s * chunk + here
        dyn[...] = jnp.zeros(dyn.shape, BF)
        for d in range(parts):
            for q in range(pairs):
                group = (s ^ d) * pairs + q
                gains[pl.ds(pl.multiple_of(group * 2 * bs, 2 * bs), 2 * bs), :] = data[d][
                    j, q, 3 * bs : 5 * bs, :
                ]
                third = data[d][j, q, 2 * bs : 3 * bs, :]
                third_turned = turn(third, bs)
                for i in range(2):
                    both = data[d][j, q, i * bs : (i + 1) * bs, :]
                    both_turned = turn(both, bs)
                    lefts = (both, both_turned, third if i == 0 else third_turned)
                    rights = (both_turned, both, third_turned if i == 0 else third)
                    row = pl.multiple_of(group * 2 * bs + i * bs, bs)
                    placed = [jnp.where(left, both, zero) if i == 0 else jnp.where(left, zero, both_turned)]
                    at = [group]
                    for e in range(1, 3):
                        column = plan_ref[d * each + e * 2 * pairs + 2 * q + i, k]
                        at.append(column >> 1)
                        placed.append(
                            jnp.where(
                                (column & 1) == 0,
                                jnp.where(left, lefts[e], zero),
                                jnp.where(left, zero, rights[e]),
                            )
                        )
                    for e in range(3):
                        value = placed[e]
                        for f in range(3):
                            if f != e:
                                value = value + jnp.where(at[e] == at[f], placed[f], zero)
                        dyn[at[e], pl.ds(row, bs), :] = value
        operator = op_ref[k].astype(F32)
        diagonal = jnp.concatenate(
            [jnp.where(left, operator, 0.0), jnp.where(left, 0.0, operator)], axis=0
        ).astype(BF)
        picks = []
        for o in range(2):
            block = plan_ref[parts * each + o, k]
            for tile in range(tiles):
                found = pl.ds(pl.multiple_of(block * bs, bs), bs)
                chosen[o * bs : (o + 1) * bs, tile * 2 * bs : (tile + 1) * 2 * bs] = (
                    dyn[tile, found, :]
                )
            row = source[block >> 1, pl.ds(here, 1), :]
            turned = pltpu.roll(row, bs, 1)
            picks.append(jnp.where((block & 1) == o, row, turned))
        image = tn(diagonal, chosen[...])
        masked = jnp.where(slot < plan_ref[parts * each + 2, k], image, 0.0).astype(BF)
        pick = jnp.where(lane_row < bs, picks[0], picks[1])
        source_image = fold(nn(split3(pick), diagonal)).astype(BF).astype(F32)
        innovation = jnp.where(
            lane_row < plan_ref[parts * each + 2, k], values_ref[pl.ds(k, 1), :] - source_image, 0.0
        )
        shift = fold(nt(split3(innovation), gains[...]))
        shift = shift + jnp.concatenate(
            [source[g, pl.ds(here, 1), :] for g in range(parts * pairs)], axis=1
        )
        offsets[j] = jnp.broadcast_to(shift, (8, ns))
        for g in range(parts * pairs):
            rows = slice(g * 2 * bs, (g + 1) * 2 * bs)
            correction = nn(gains[rows, :], masked)
            for tile in range(tiles):
                lanes = slice(tile * 2 * bs, (tile + 1) * 2 * bs)
                forward = dyn[tile, rows, :].astype(F32)
                elements[j, rows, lanes] = (forward - correction[:, lanes]).astype(BF)
    if first == 0:
        begin = jnp.logical_and(s == 0, tm_ref[0] == 0)
        vec = jnp.where(begin, prior_ref[...], 0.0)
    else:
        vec = vec_in[...]
    for j in range(count):
        element = elements[j]
        vec = fold(nt(split3(vec), element)) + offsets[j, 0:1, :]
        held = map_in if j == 0 else map_ref
        for r in range(0, ns, step_of(ns)):
            rows, below = slice(r, r + step_of(ns)), slice(ns + r, ns + r + step_of(ns))
            if first == 0 and j == 0:
                across = lax.broadcasted_iota(jnp.int32, (step_of(ns), ns), 1)
                down = lax.broadcasted_iota(jnp.int32, (step_of(ns), ns), 0) + r
                unit = jnp.where(across == down, 1.0, 0.0).astype(BF)
                map_ref[rows, :] = nt(unit, element).astype(BF)
                continue
            moved = nt(held[rows, :], element)
            if first > 0 or j > 1:
                moved = moved + nt(held[below, :], element)
            top = moved.astype(BF)
            map_ref[rows, :] = top
            map_ref[below, :] = (moved - top.astype(F32)).astype(BF)
    vec_ref[...] = vec


def chunk_piece(
    position, span, plan, data, small, obs_op, obs_values, prior, state, chunk, first, count
):
    parts = len(data)
    pairs, _, width = data[0].shape[1:]
    bs = width // 2
    ns = parts * pairs * width
    if state is None:
        state = (data[0], prior)
    return pl.pallas_call(
        functools.partial(chunk_kernel, parts, pairs, bs, chunk, first, count),
        grid_spec=pltpu.PrefetchScalarGridSpec(
            num_scalar_prefetch=3,
            grid=(),
            in_specs=vmem(2 * parts + 5),
            out_specs=vmem(4),
            scratch_shapes=[
                pltpu.VMEM((parts * pairs, ns, width), BF),
                pltpu.VMEM((ns, width), BF),
                pltpu.VMEM((parts * pairs, chunk, width), F32),
                pltpu.VMEM((width, ns), BF),
            ],
        ),
        out_shape=[
            jax.ShapeDtypeStruct((count, ns, ns), BF),
            jax.ShapeDtypeStruct((count, 8, ns), F32),
            jax.ShapeDtypeStruct((2 * ns, ns), BF),
            jax.ShapeDtypeStruct((1, ns), F32),
        ],
        compiler_params=pltpu.CompilerParams(vmem_limit_bytes=VMEM_LIMIT),
    )(
        position, span, plan, *data, *small, obs_op, obs_values, prior, *state,
    )


def apply_map(row, held):
    ns = held.shape[1]
    parts = split3(row)
    return fold(nn(parts, held[:ns, :]) + nn(parts, held[ns : 2 * ns, :]))


def join_kernel(one, two, vec_ref, out_ref):
    ns = one.shape[1]
    for r in range(0, ns, step_of(ns)):
        rows, below = slice(r, r + step_of(ns)), slice(ns + r, ns + r + step_of(ns))
        product = nn(one[rows, :], two[:ns, :]) + (
            nn(one[rows, :], two[ns : 2 * ns, :]) + nn(one[below, :], two[:ns, :])
        )
        top = product.astype(BF)
        out_ref[rows, :] = top
        out_ref[below, :] = (product - top.astype(F32)).astype(BF)
    out_ref[2 * ns :, :] = split3(vec_ref[...])


def join(one, two, vec):
    ns = one.shape[1]
    return pl.pallas_call(
        join_kernel,
        in_specs=vmem(3),
        out_specs=vmem(1)[0],
        out_shape=jax.ShapeDtypeStruct((2 * ns + ROWS, ns), BF),
        compiler_params=pltpu.CompilerParams(vmem_limit_bytes=VMEM_LIMIT),
        name="join",
    )(one, two, vec)


def hop_kernel(row_ref, *refs):
    current, out_ref = row_ref[...], refs[-1]
    for n in range(0, len(refs) - 1, 2):
        current = apply_map(current, refs[n]) + refs[n + 1][...]
    out_ref[...] = current


def hop(row, *maps):
    return pl.pallas_call(
        hop_kernel,
        in_specs=vmem(1 + len(maps)),
        out_specs=vmem(1)[0],
        out_shape=jax.ShapeDtypeStruct(row.shape, F32),
        compiler_params=pltpu.CompilerParams(vmem_limit_bytes=VMEM_LIMIT),
        name="hop",
    )(row, *maps)


def span_kernel(leaders, whole, early, s_ref, tm_ref, row_ref, direct_ref, *refs):
    maps, out_ref = refs[:leaders], refs[leaders]
    ns = out_ref.shape[1]
    for mine in range(leaders):

        @pl.when(s_ref[0] // 2 == mine)
        def _():
            current = row_ref[...]
            for p in range(leaders if whole else mine):
                held = maps[p ^ mine]
                current = apply_map(current, held) + fold(held[2 * ns :, :].astype(F32))
            if not whole:
                current = jnp.where(tm_ref[0] < early, direct_ref[...], current)
            out_ref[...] = current


def span_hop(position, span, row, direct, maps, whole, early):
    leaders = len(maps)
    return pl.pallas_call(
        functools.partial(span_kernel, leaders, whole, early),
        grid_spec=pltpu.PrefetchScalarGridSpec(
            num_scalar_prefetch=2,
            grid=(),
            in_specs=vmem(2 + leaders),
            out_specs=vmem(1)[0],
        ),
        out_shape=jax.ShapeDtypeStruct(row.shape, F32),
        compiler_params=pltpu.CompilerParams(vmem_limit_bytes=VMEM_LIMIT),
        name="span_hop" if whole else "lead",
    )(position, span, row, direct, *maps)


def sweep_kernel(pieces, parts, s_ref, tm_ref, *refs):
    own_ref, told_ref, prior_ref, map_ref, vec_ref = refs[:5]
    refs = refs[5:]
    elements, offsets = refs[:pieces], refs[pieces : 2 * pieces]
    outs = refs[2 * pieces : 2 * pieces + parts]
    current_ref, spread = refs[2 * pieces + parts :]
    s = s_ref[0]
    begin = jnp.logical_and(s == 0, tm_ref[0] == 0)

    @pl.when(s % 2 == 0)
    def _():
        current_ref[...] = told_ref[...] + jnp.where(begin, prior_ref[...], 0.0)

    @pl.when(s % 2 == 1)
    def _():
        current_ref[...] = apply_map(own_ref[...], map_ref) + vec_ref[...]

    current = current_ref[...]
    at = 0
    width = spread.shape[2]
    for p in range(pieces):
        for j in range(elements[p].shape[0]):
            current = fold(nt(split3(current), elements[p][j])) + offsets[p][j, 0:1, :]
            for d in range(parts):
                spread[d, at : at + 1, :] = current[:, d * width : (d + 1) * width]
            at += 1
    for d in range(parts):
        outs[d][...] = spread[s ^ d]


def sweep(position, span, own, told, prior, even, elements, offsets, parts):
    ns = own.shape[1]
    pieces = len(elements)
    chunk = sum(e.shape[0] for e in elements)
    width = ns // parts
    return pl.pallas_call(
        functools.partial(sweep_kernel, pieces, parts),
        grid_spec=pltpu.PrefetchScalarGridSpec(
            num_scalar_prefetch=2,
            grid=(),
            in_specs=vmem(5 + 2 * pieces),
            out_specs=vmem(parts),
            scratch_shapes=[
                pltpu.VMEM((1, ns), F32),
                pltpu.VMEM((parts, chunk, width), F32),
            ],
        ),
        out_shape=[jax.ShapeDtypeStruct((chunk, width), F32)] * parts,
        compiler_params=pltpu.CompilerParams(vmem_limit_bytes=VMEM_LIMIT),
        name="sweep",
    )(position, span, own, told, prior, *even, *elements, *offsets)


def gather_kernel(parts, s_ref, *refs):
    blocks, out_ref = refs[:parts], refs[parts]
    rows = blocks[0].shape[0]
    for d in range(parts):
        out_ref[pl.ds(pl.multiple_of((s_ref[0] ^ d) * rows, rows), rows), :] = blocks[d][...]


def gather(position, blocks):
    rows, width = blocks[0].shape
    parts = len(blocks)
    return pl.pallas_call(
        functools.partial(gather_kernel, parts),
        grid_spec=pltpu.PrefetchScalarGridSpec(
            num_scalar_prefetch=1, grid=(), in_specs=vmem(parts), out_specs=vmem(1)[0]
        ),
        out_shape=jax.ShapeDtypeStruct((parts * rows, width), F32),
        compiler_params=pltpu.CompilerParams(vmem_limit_bytes=VMEM_LIMIT),
        name="gather",
    )(position, *blocks)


PIECES = 5


def piece_sizes(chunk):
    base, more = divmod(chunk - 2, PIECES - 2)
    return [base + 1] * more + [base] * (PIECES - 2 - more) + [1, 1]


def means(dyn_cols, dyn_vals, obs_blocks, obs_op, obs_counts, obs_values, gain, sources, prior):
    steps, _, _, _ = dyn_vals.shape
    parts = lax.axis_size("state")
    spans = lax.axis_size("tm")
    chunk = steps // parts
    ns = prior.shape[0]
    s = lax.axis_index("state")
    t = lax.axis_index("tm")
    position = s.reshape(1).astype(jnp.int32)
    span = t.reshape(1).astype(jnp.int32)
    prior_row = prior.reshape(1, ns)

    def across(x, d):
        return lax.ppermute(x, "state", [(i, i ^ d) for i in range(parts)])

    def send(x, pairs):
        return lax.ppermute(x, ("tm", "state"), [(a * parts + b, c * parts + e) for (a, b), (c, e) in pairs])

    order = sorted(range(1, parts), reverse=True)
    sizes = piece_sizes(chunk)
    firsts = [sum(sizes[:n]) for n in range(len(sizes))]
    vals_far = pltpu.with_memory_space_constraint(dyn_vals, pltpu.HBM)
    gain_far = pltpu.with_memory_space_constraint(gain, pltpu.HBM)
    pieces = []
    for n, (first, size) in enumerate(zip(firsts, sizes)):
        source_arrays = (vals_far, gain_far) if n == 0 else (dyn_vals, gain)
        table = (sources, dyn_cols.transpose(2, 1, 0)) if n == 1 else ()
        packed = pack(position, span, *source_arrays, parts, chunk, first, size, table)
        arrived = {0: packed[0]}
        for d in order:
            arrived[d] = across(packed[d], d)
        pieces.append([arrived[d] for d in range(parts)])
        if n == 1:
            small = {0: packed[parts]}
            for d in order:
                small[d] = across(packed[parts + d], d)
            small = [small[d] for d in range(parts)]

    plan = plan_of(small, obs_blocks.T, obs_counts.reshape(1, steps), chunk)
    state = None
    elements, offsets = [], []
    for first, size, data in zip(firsts, sizes, pieces):
        element, offset, *state = chunk_piece(
            position, span, plan, data, small, obs_op, obs_values,
            prior_row, state, chunk, first, size,
        )
        elements.append(element)
        offsets.append(offset)
    chunk_map, vec = state

    leads = [2 * p + 1 for p in range(parts // 2)]
    to_lead = [((a, l - 1), (a, l)) for a in range(spans) for l in leads]
    vec_even = send(vec, to_lead)
    map_even = send(chunk_map, to_lead)
    both = (map_even, vec_even, chunk_map, vec)
    pair_vec = hop(vec_even, chunk_map, vec)
    pair = join(map_even, chunk_map, pair_vec)

    early = min(2, spans - 1)
    maps = [pair]
    for d in range(2, parts, 2):
        pairs = [((a, l), (a, l ^ d)) for a in range(early, spans) for l in leads]
        maps.append(send(pair, pairs))

    direct = jnp.zeros((1, ns), F32)
    entry = jnp.zeros((1, ns), F32)
    current = pair_vec
    for g in range(early):
        for p in range(1, len(leads)):
            arriving = send(current, [((g, leads[p - 1]), (g, leads[p]))])
            direct = direct + arriving
            current = hop(arriving, *both)
        if g + 1 < early:
            arriving = send(current, [((g, leads[-1]), (g + 1, leads[0]))])
            direct = direct + arriving
            current = hop(arriving, *both)
        else:
            for l in leads:
                entry = entry + send(current, [((g, leads[-1]), (g + 1, l))])

    arriving = entry
    for h in range(early, spans - 1):
        current = span_hop(position, span, arriving, direct, maps, True, early)
        arriving = send(current, [((h, l), (h + 1, l)) for l in leads])
        entry = entry + arriving

    own = span_hop(position, span, entry, direct, maps, False, early)
    told = send(own, [(b, a) for a, b in to_lead])
    mine = sweep(
        position, span, own, told, prior_row, (map_even, vec_even), elements, offsets, parts
    )
    got = {0: mine[0]}
    for d in order:
        got[d] = across(mine[d], d)
    return gather(position, [got[d] for d in range(parts)])


def solution(mesh):
    return jax.shard_map(
        means,
        mesh=mesh,
        in_specs=(
            P("tm", "state", None),
            P("tm", "state", None, None),
            P("tm", None),
            P("tm", None, None),
            P("tm"),
            P("tm", None),
            P("tm", "state", None),
            P("tm", "state"),
            P(),
        ),
        out_specs=P("tm", "state"),
        check_vma=False,
    )
```

```python
import functools

import jax
import jax.numpy as jnp
from jax import lax
from jax.experimental import pallas as pl
from jax.experimental.pallas import tpu as pltpu
from jax.sharding import PartitionSpec as P


BF = jnp.bfloat16
F32 = jnp.float32
VMEM_LIMIT = 12 * 1024 * 1024
ROWS = 16


def nt(a, b):
    return lax.dot_general(a, b, (((1,), (1,)), ((), ())), preferred_element_type=F32)


def nn(a, b):
    return lax.dot_general(a, b, (((1,), (0,)), ((), ())), preferred_element_type=F32)


def tn(a, b):
    return lax.dot_general(a, b, (((0,), (0,)), ((), ())), preferred_element_type=F32)


def split3(row):
    hi = row.astype(BF).astype(F32)
    rest = row - hi
    mid = rest.astype(BF).astype(F32)
    low = rest - mid
    at = lax.broadcasted_iota(jnp.int32, (ROWS, row.shape[1]), 0)
    zero = jnp.zeros((), F32)
    return jnp.where(at == 0, hi, jnp.where(at == 1, mid, jnp.where(at == 2, low, zero))).astype(BF)


def step_of(ns):
    return 256 if ns % 256 == 0 else ns


def turn(block, by):
    return jnp.concatenate([block[:, by:], block[:, :by]], axis=1)


def fold(rows):
    return jnp.sum(rows, axis=0, keepdims=True)


def vmem(n):
    return [pl.BlockSpec(memory_space=pltpu.VMEM)] * n


def pack_kernel(parts, pairs, bs, chunk, table, s_ref, tm_ref, *refs):
    vals, gains = refs[:parts], refs[parts : 2 * parts]
    refs = refs[2 * parts :]
    if table:
        source_ref, cols_ref = refs[:2]
        refs = refs[2:]
        tables = refs[parts:]
        for d in range(parts):
            tables[d][...] = jnp.zeros(tables[d].shape, F32)
            begin = pl.multiple_of((s_ref[0] ^ d) * chunk, chunk)
            tables[d][:chunk, :] = source_ref[pl.ds(begin, chunk), :]
            for e in range(cols_ref.shape[0]):
                for i in range(cols_ref.shape[1]):
                    at = chunk + e * cols_ref.shape[1] + i
                    line = cols_ref[e, i : i + 1, :].astype(F32)
                    tables[d][at : at + 1, : line.shape[1]] = line
    outs = refs[:parts]
    for d in range(parts):
        for q in range(pairs):
            for i in range(2):
                outs[d][0, q, i * bs : (i + 1) * bs, :] = vals[d][0, 2 * q + i, :, : 2 * bs]
            base = 2 * bs
            third = jnp.concatenate(
                [vals[d][0, 2 * q, :, 2 * bs :], vals[d][0, 2 * q + 1, :, 2 * bs :]], axis=1
            )
            outs[d][0, q, base : base + bs, :] = third
            base = 3 * bs
            outs[d][0, q, base : base + 2 * bs, :] = gains[d][0, q * 2 * bs : (q + 1) * 2 * bs, :]


def pack(position, span, dyn_vals, gain, parts, chunk, first, count, table=()):
    _, lb, bs, width = dyn_vals.shape
    rows, obs = gain.shape[1:]
    pairs = lb // 2

    def from_part(d, trail):
        return lambda j, s, t: ((s[0] ^ d) * chunk + first + j,) + (0,) * trail

    shape = (count, pairs, 5 * bs, 2 * bs)
    tables = [jax.ShapeDtypeStruct((chunk + 3 * lb, lb * bs), F32)] * (parts if table else 0)
    return pl.pallas_call(
        functools.partial(pack_kernel, parts, pairs, bs, chunk, bool(table)),
        grid_spec=pltpu.PrefetchScalarGridSpec(
            num_scalar_prefetch=2,
            grid=(count,),
            in_specs=[pl.BlockSpec((1, lb, bs, width), from_part(d, 3)) for d in range(parts)]
            + [pl.BlockSpec((1, rows, obs), from_part(d, 2)) for d in range(parts)]
            + vmem(len(table)),
            out_specs=[pl.BlockSpec((1,) + shape[1:], lambda j, s, t: (j, 0, 0, 0))] * parts
            + vmem(len(tables)),
        ),
        out_shape=[jax.ShapeDtypeStruct(shape, BF)] * parts + tables,
        compiler_params=pltpu.CompilerParams(vmem_limit_bytes=VMEM_LIMIT),
    )(position, span, *([dyn_vals] * parts), *([gain] * parts), *table)


def plan_kernel(parts, chunk, *refs):
    small, blocks, counts, out_ref = refs[:parts], refs[parts], refs[parts + 1], refs[parts + 2]
    steps = counts.shape[1]
    each = small[0].shape[0] - chunk
    for d in range(parts):
        out_ref[d * each : (d + 1) * each, :] = small[d][chunk:, :steps].astype(jnp.int32)
    out_ref[parts * each : parts * each + 2, :] = blocks[...]
    out_ref[parts * each + 2 : parts * each + 3, :] = counts[...]


def plan_of(small, blocks, counts, chunk):
    parts = len(small)
    each = small[0].shape[0] - chunk
    return pl.pallas_call(
        functools.partial(plan_kernel, parts, chunk),
        in_specs=vmem(parts + 2),
        out_specs=vmem(1)[0],
        out_shape=jax.ShapeDtypeStruct((parts * each + 3, counts.shape[1]), jnp.int32),
        compiler_params=pltpu.CompilerParams(vmem_limit_bytes=VMEM_LIMIT),
        name="plan",
    )(*small, blocks, counts)


def chunk_kernel(
    parts, pairs, bs, chunk, first, count, s_ref, tm_ref, plan_ref, *refs
):
    each = 6 * pairs
    data, small = refs[:parts], refs[parts : 2 * parts]
    op_ref, values_ref, prior_ref, map_in, vec_in = refs[2 * parts : 2 * parts + 5]
    elements, offsets, map_ref, vec_ref = refs[2 * parts + 5 : 2 * parts + 9]
    dyn, gains, source, chosen = refs[2 * parts + 9 :]
    s = s_ref[0]
    ns = parts * pairs * 2 * bs
    lane = lax.broadcasted_iota(jnp.int32, (bs, 2 * bs), 1)
    left = lane < bs
    zero = jnp.zeros((), BF)
    tiles = parts * pairs
    lane_row = lax.broadcasted_iota(jnp.int32, (1, 2 * bs), 1)
    slot = lax.broadcasted_iota(jnp.int32, (2 * bs, 1), 0)
    for d in range(parts):
        for q in range(pairs):
            source[(s ^ d) * pairs + q] = small[d][:chunk, q * 2 * bs : (q + 1) * 2 * bs]
    for j in range(count):
        here = first + j
        k = s * chunk + here
        dyn[...] = jnp.zeros(dyn.shape, BF)
        for d in range(parts):
            for q in range(pairs):
                group = (s ^ d) * pairs + q
                gains[pl.ds(pl.multiple_of(group * 2 * bs, 2 * bs), 2 * bs), :] = data[d][
                    j, q, 3 * bs : 5 * bs, :
                ]
                third = data[d][j, q, 2 * bs : 3 * bs, :]
                third_turned = turn(third, bs)
                for i in range(2):
                    both = data[d][j, q, i * bs : (i + 1) * bs, :]
                    both_turned = turn(both, bs)
                    lefts = (both, both_turned, third if i == 0 else third_turned)
                    rights = (both_turned, both, third_turned if i == 0 else third)
                    row = pl.multiple_of(group * 2 * bs + i * bs, bs)
                    placed = [jnp.where(left, both, zero) if i == 0 else jnp.where(left, zero, both_turned)]
                    at = [group]
                    for e in range(1, 3):
                        column = plan_ref[d * each + e * 2 * pairs + 2 * q + i, k]
                        at.append(column >> 1)
                        placed.append(
                            jnp.where(
                                (column & 1) == 0,
                                jnp.where(left, lefts[e], zero),
                                jnp.where(left, zero, rights[e]),
                            )
                        )
                    for e in range(3):
                        value = placed[e]
                        for f in range(3):
                            if f != e:
                                value = value + jnp.where(at[e] == at[f], placed[f], zero)
                        dyn[at[e], pl.ds(row, bs), :] = value
        operator = op_ref[k].astype(F32)
        diagonal = jnp.concatenate(
            [jnp.where(left, operator, 0.0), jnp.where(left, 0.0, operator)], axis=0
        ).astype(BF)
        picks = []
        for o in range(2):
            block = plan_ref[parts * each + o, k]
            for tile in range(tiles):
                found = pl.ds(pl.multiple_of(block * bs, bs), bs)
                chosen[o * bs : (o + 1) * bs, tile * 2 * bs : (tile + 1) * 2 * bs] = (
                    dyn[tile, found, :]
                )
            row = source[block >> 1, pl.ds(here, 1), :]
            turned = pltpu.roll(row, bs, 1)
            picks.append(jnp.where((block & 1) == o, row, turned))
        image = tn(diagonal, chosen[...])
        masked = jnp.where(slot < plan_ref[parts * each + 2, k], image, 0.0).astype(BF)
        pick = jnp.where(lane_row < bs, picks[0], picks[1])
        source_image = fold(nn(split3(pick), diagonal)).astype(BF).astype(F32)
        innovation = jnp.where(
            lane_row < plan_ref[parts * each + 2, k], values_ref[pl.ds(k, 1), :] - source_image, 0.0
        )
        shift = fold(nt(split3(innovation), gains[...]))
        shift = shift + jnp.concatenate(
            [source[g, pl.ds(here, 1), :] for g in range(parts * pairs)], axis=1
        )
        offsets[j] = jnp.broadcast_to(shift, (8, ns))
        for g in range(parts * pairs):
            rows = slice(g * 2 * bs, (g + 1) * 2 * bs)
            correction = nn(gains[rows, :], masked)
            for tile in range(tiles):
                lanes = slice(tile * 2 * bs, (tile + 1) * 2 * bs)
                forward = dyn[tile, rows, :].astype(F32)
                elements[j, rows, lanes] = (forward - correction[:, lanes]).astype(BF)
    if first == 0:
        begin = jnp.logical_and(s == 0, tm_ref[0] == 0)
        vec = jnp.where(begin, prior_ref[...], 0.0)
    else:
        vec = vec_in[...]
    for j in range(count):
        element = elements[j]
        vec = fold(nt(split3(vec), element)) + offsets[j, 0:1, :]
        held = map_in if j == 0 else map_ref
        for r in range(0, ns, step_of(ns)):
            rows, below = slice(r, r + step_of(ns)), slice(ns + r, ns + r + step_of(ns))
            if first == 0 and j == 0:
                across = lax.broadcasted_iota(jnp.int32, (step_of(ns), ns), 1)
                down = lax.broadcasted_iota(jnp.int32, (step_of(ns), ns), 0) + r
                unit = jnp.where(across == down, 1.0, 0.0).astype(BF)
                map_ref[rows, :] = nt(unit, element).astype(BF)
                map_ref[below, :] = jnp.zeros((step_of(ns), ns), BF)
                continue
            moved = nt(held[rows, :], element)
            if first > 0 or j > 1:
                moved = moved + nt(held[below, :], element)
            top = moved.astype(BF)
            map_ref[rows, :] = top
            map_ref[below, :] = (moved - top.astype(F32)).astype(BF)
    vec_ref[...] = vec
    map_ref[2 * ns :, :] = split3(vec)


def chunk_piece(
    position, span, plan, data, small, obs_op, obs_values, prior, state, chunk, first, count
):
    parts = len(data)
    pairs, _, width = data[0].shape[1:]
    bs = width // 2
    ns = parts * pairs * width
    if state is None:
        state = (data[0], prior)
    return pl.pallas_call(
        functools.partial(chunk_kernel, parts, pairs, bs, chunk, first, count),
        grid_spec=pltpu.PrefetchScalarGridSpec(
            num_scalar_prefetch=3,
            grid=(),
            in_specs=vmem(2 * parts + 5),
            out_specs=vmem(4),
            scratch_shapes=[
                pltpu.VMEM((parts * pairs, ns, width), BF),
                pltpu.VMEM((ns, width), BF),
                pltpu.VMEM((parts * pairs, chunk, width), F32),
                pltpu.VMEM((width, ns), BF),
            ],
        ),
        out_shape=[
            jax.ShapeDtypeStruct((count, ns, ns), BF),
            jax.ShapeDtypeStruct((count, 8, ns), F32),
            jax.ShapeDtypeStruct((2 * ns + ROWS, ns), BF),
            jax.ShapeDtypeStruct((1, ns), F32),
        ],
        compiler_params=pltpu.CompilerParams(vmem_limit_bytes=VMEM_LIMIT),
    )(
        position, span, plan, *data, *small, obs_op, obs_values, prior, *state,
    )


def apply_map(row, held):
    ns = held.shape[1]
    parts = split3(row)
    moved = fold(nn(parts, held[:ns, :]) + nn(parts, held[ns : 2 * ns, :]))
    return moved + fold(held[2 * ns :, :].astype(F32))


def join_kernel(one, two, out_ref):
    ns = one.shape[1]
    for r in range(0, ns, step_of(ns)):
        rows, below = slice(r, r + step_of(ns)), slice(ns + r, ns + r + step_of(ns))
        product = nn(one[rows, :], two[:ns, :]) + (
            nn(one[rows, :], two[ns : 2 * ns, :]) + nn(one[below, :], two[:ns, :])
        )
        top = product.astype(BF)
        out_ref[rows, :] = top
        out_ref[below, :] = (product - top.astype(F32)).astype(BF)
    out_ref[2 * ns :, :] = split3(apply_map(fold(one[2 * ns :, :].astype(F32)), two))


def join(one, two):
    return pl.pallas_call(
        join_kernel,
        in_specs=vmem(2),
        out_specs=vmem(1)[0],
        out_shape=jax.ShapeDtypeStruct(two.shape, BF),
        compiler_params=pltpu.CompilerParams(vmem_limit_bytes=VMEM_LIMIT),
        name="join",
    )(one, two)


def hop_kernel(row_ref, *refs):
    current = row_ref[...]
    for held in refs[:-1]:
        current = apply_map(current, held)
    refs[-1][...] = current


def hop(row, *maps):
    return pl.pallas_call(
        hop_kernel,
        in_specs=vmem(1 + len(maps)),
        out_specs=vmem(1)[0],
        out_shape=jax.ShapeDtypeStruct(row.shape, F32),
        compiler_params=pltpu.CompilerParams(vmem_limit_bytes=VMEM_LIMIT),
        name="hop",
    )(row, *maps)


def span_kernel(leaders, s_ref, row_ref, *refs):
    maps, out_ref = refs[:leaders], refs[leaders]
    for mine in range(leaders):

        @pl.when(s_ref[0] // 2 == mine)
        def _():
            current = row_ref[...]
            for p in range(leaders):
                current = apply_map(current, maps[p ^ mine])
            out_ref[...] = current


def span_hop(position, row, maps):
    leaders = len(maps)
    return pl.pallas_call(
        functools.partial(span_kernel, leaders),
        grid_spec=pltpu.PrefetchScalarGridSpec(
            num_scalar_prefetch=1,
            grid=(),
            in_specs=vmem(1 + leaders),
            out_specs=vmem(1)[0],
        ),
        out_shape=jax.ShapeDtypeStruct(row.shape, F32),
        compiler_params=pltpu.CompilerParams(vmem_limit_bytes=VMEM_LIMIT),
        name="span_hop",
    )(position, row, *maps)


def lead_kernel(leaders, early, s_ref, tm_ref, row_ref, direct_ref, *refs):
    sets, out_ref = (refs[:leaders], refs[leaders : 2 * leaders]), refs[2 * leaders]

    @pl.when(tm_ref[0] < early)
    def _():
        out_ref[...] = direct_ref[...]

    for mine in range(leaders):
        for late in range(2):
            reached = (tm_ref[0] > early) if late else (tm_ref[0] == early)

            @pl.when(jnp.logical_and(s_ref[0] // 2 == mine, reached))
            def _():
                current = row_ref[...]
                for p in range(mine):
                    current = apply_map(current, sets[late][p ^ mine])
                out_ref[...] = current


def lead(position, span, row, direct, maps, maps_late, early):
    leaders = len(maps)
    return pl.pallas_call(
        functools.partial(lead_kernel, leaders, early),
        grid_spec=pltpu.PrefetchScalarGridSpec(
            num_scalar_prefetch=2,
            grid=(),
            in_specs=vmem(2 + 2 * leaders),
            out_specs=vmem(1)[0],
        ),
        out_shape=jax.ShapeDtypeStruct(row.shape, F32),
        compiler_params=pltpu.CompilerParams(vmem_limit_bytes=VMEM_LIMIT),
        name="lead",
    )(position, span, row, direct, *maps, *maps_late)


def sweep_kernel(pieces, parts, s_ref, tm_ref, *refs):
    own_ref, told_ref, prior_ref, first_map, first_vec, map_ref = refs[:6]
    refs = refs[6:]
    elements, offsets = refs[:pieces], refs[pieces : 2 * pieces]
    outs = refs[2 * pieces : 2 * pieces + parts]
    current_ref, spread = refs[2 * pieces + parts :]
    s = s_ref[0]
    begin = jnp.logical_and(s == 0, tm_ref[0] == 0)

    @pl.when(s % 2 == 0)
    def _():
        current_ref[...] = told_ref[...] + jnp.where(begin, prior_ref[...], 0.0)

    @pl.when(jnp.logical_and(s % 2 == 1, tm_ref[0] == 0))
    def _():
        current_ref[...] = apply_map(own_ref[...], first_map) + first_vec[...]

    @pl.when(jnp.logical_and(s % 2 == 1, tm_ref[0] > 0))
    def _():
        current_ref[...] = apply_map(own_ref[...], map_ref)

    current = current_ref[...]
    at = 0
    width = spread.shape[2]
    for p in range(pieces):
        for j in range(elements[p].shape[0]):
            current = fold(nt(split3(current), elements[p][j])) + offsets[p][j, 0:1, :]
            for d in range(parts):
                spread[d, at : at + 1, :] = current[:, d * width : (d + 1) * width]
            at += 1
    for d in range(parts):
        outs[d][...] = spread[s ^ d]


def sweep(position, span, own, told, prior, even, elements, offsets, parts):
    ns = own.shape[1]
    pieces = len(elements)
    chunk = sum(e.shape[0] for e in elements)
    width = ns // parts
    return pl.pallas_call(
        functools.partial(sweep_kernel, pieces, parts),
        grid_spec=pltpu.PrefetchScalarGridSpec(
            num_scalar_prefetch=2,
            grid=(),
            in_specs=vmem(6 + 2 * pieces),
            out_specs=vmem(parts),
            scratch_shapes=[
                pltpu.VMEM((1, ns), F32),
                pltpu.VMEM((parts, chunk, width), F32),
            ],
        ),
        out_shape=[jax.ShapeDtypeStruct((chunk, width), F32)] * parts,
        compiler_params=pltpu.CompilerParams(vmem_limit_bytes=VMEM_LIMIT),
        name="sweep",
    )(position, span, own, told, prior, *even, *elements, *offsets)


def gather_kernel(parts, s_ref, *refs):
    blocks, out_ref = refs[:parts], refs[parts]
    rows = blocks[0].shape[0]
    for d in range(parts):
        out_ref[pl.ds(pl.multiple_of((s_ref[0] ^ d) * rows, rows), rows), :] = blocks[d][...]


def gather(position, blocks):
    rows, width = blocks[0].shape
    parts = len(blocks)
    return pl.pallas_call(
        functools.partial(gather_kernel, parts),
        grid_spec=pltpu.PrefetchScalarGridSpec(
            num_scalar_prefetch=1, grid=(), in_specs=vmem(parts), out_specs=vmem(1)[0]
        ),
        out_shape=jax.ShapeDtypeStruct((parts * rows, width), F32),
        compiler_params=pltpu.CompilerParams(vmem_limit_bytes=VMEM_LIMIT),
        name="gather",
    )(position, *blocks)


PIECES = 5


def piece_sizes(chunk):
    base, more = divmod(chunk - 2, PIECES - 2)
    return [base + 1] * more + [base] * (PIECES - 2 - more) + [1, 1]


def means(dyn_cols, dyn_vals, obs_blocks, obs_op, obs_counts, obs_values, gain, sources, prior):
    steps, _, _, _ = dyn_vals.shape
    parts = lax.axis_size("state")
    spans = lax.axis_size("tm")
    chunk = steps // parts
    ns = prior.shape[0]
    s = lax.axis_index("state")
    t = lax.axis_index("tm")
    position = s.reshape(1).astype(jnp.int32)
    span = t.reshape(1).astype(jnp.int32)
    prior_row = prior.reshape(1, ns)

    def across(x, d):
        return lax.ppermute(x, "state", [(i, i ^ d) for i in range(parts)])

    def send(x, pairs):
        return lax.ppermute(x, ("tm", "state"), [(a * parts + b, c * parts + e) for (a, b), (c, e) in pairs])

    order = sorted(range(1, parts), reverse=True)
    sizes = piece_sizes(chunk)
    firsts = [sum(sizes[:n]) for n in range(len(sizes))]
    vals_far = pltpu.with_memory_space_constraint(dyn_vals, pltpu.HBM)
    gain_far = pltpu.with_memory_space_constraint(gain, pltpu.HBM)
    pieces = []
    for n, (first, size) in enumerate(zip(firsts, sizes)):
        source_arrays = (vals_far, gain_far) if n == 0 else (dyn_vals, gain)
        table = (sources, dyn_cols.transpose(2, 1, 0)) if n == 1 else ()
        packed = pack(position, span, *source_arrays, parts, chunk, first, size, table)
        arrived = {0: packed[0]}
        for d in order:
            arrived[d] = across(packed[d], d)
        pieces.append([arrived[d] for d in range(parts)])
        if n == 1:
            small = {0: packed[parts]}
            for d in order:
                small[d] = across(packed[parts + d], d)
            small = [small[d] for d in range(parts)]

    plan = plan_of(small, obs_blocks.T, obs_counts.reshape(1, steps), chunk)
    state = None
    elements, offsets = [], []
    for first, size, data in zip(firsts, sizes, pieces):
        element, offset, *state = chunk_piece(
            position, span, plan, data, small, obs_op, obs_values,
            prior_row, state, chunk, first, size,
        )
        elements.append(element)
        offsets.append(offset)
    chunk_map, vec = state

    leads = [2 * p + 1 for p in range(parts // 2)]
    to_lead = [((a, l - 1), (a, l)) for a in range(spans) for l in leads]
    map_even = send(chunk_map, [pair for pair in to_lead if pair[0][0] > 0])
    first_vec = send(vec, to_lead[:1])
    first_map = send(chunk_map, to_lead[1 : len(leads)])
    current = hop(first_vec, chunk_map)
    pair = join(map_even, chunk_map)

    early = min(2, spans - 1)
    maps, maps_late = [pair], [pair]
    for d in range(2, parts, 2):
        pairs = [((a, l), (a, l ^ d)) for a in range(early, spans) for l in leads]
        maps.append(send(pair, pairs[: len(leads)]))
        maps_late.append(send(pair, pairs[len(leads) :]))

    direct = jnp.zeros((1, ns), F32)
    entry = jnp.zeros((1, ns), F32)
    for g in range(early):
        held = (pair,) if g > 0 else (first_map, chunk_map)
        for p in range(1, len(leads)):
            arriving = send(current, [((g, leads[p - 1]), (g, leads[p]))])
            direct = direct + arriving
            current = hop(arriving, *held)
        if g + 1 < early:
            arriving = send(current, [((g, leads[-1]), (g + 1, leads[0]))])
            direct = direct + arriving
            current = hop(arriving, pair)
        else:
            for l in leads:
                entry = entry + send(current, [((g, leads[-1]), (g + 1, l))])

    arriving = entry
    for h in range(early, spans - 1):
        current = span_hop(position, arriving, maps if h == early else maps_late)
        arriving = send(current, [((h, l), (h + 1, l)) for l in leads])
        entry = entry + arriving

    own = lead(position, span, entry, direct, maps, maps_late, early)
    told = send(own, [(b, a) for a, b in to_lead])
    mine = sweep(
        position, span, own, told, prior_row, (first_map, first_vec, map_even), elements, offsets, parts,
    )
    got = {0: mine[0]}
    for d in order:
        got[d] = across(mine[d], d)
    return gather(position, [got[d] for d in range(parts)])


def solution(mesh):
    return jax.shard_map(
        means,
        mesh=mesh,
        in_specs=(
            P("tm", "state", None),
            P("tm", "state", None, None),
            P("tm", None),
            P("tm", None, None),
            P("tm"),
            P("tm", None),
            P("tm", "state", None),
            P("tm", "state"),
            P(),
        ),
        out_specs=P("tm", "state"),
        check_vma=False,
    )
```

```python
import functools

import jax
import jax.numpy as jnp
from jax import lax
from jax.experimental import pallas as pl
from jax.experimental.pallas import tpu as pltpu
from jax.sharding import PartitionSpec as P


BF = jnp.bfloat16
F32 = jnp.float32
VMEM_LIMIT = 12 * 1024 * 1024
ROWS = 16


def nt(a, b):
    return lax.dot_general(a, b, (((1,), (1,)), ((), ())), preferred_element_type=F32)


def nn(a, b):
    return lax.dot_general(a, b, (((1,), (0,)), ((), ())), preferred_element_type=F32)


def tn(a, b):
    return lax.dot_general(a, b, (((0,), (0,)), ((), ())), preferred_element_type=F32)


def split3(row):
    hi = row.astype(BF).astype(F32)
    rest = row - hi
    mid = rest.astype(BF).astype(F32)
    low = rest - mid
    at = lax.broadcasted_iota(jnp.int32, (ROWS, row.shape[1]), 0)
    zero = jnp.zeros((), F32)
    return jnp.where(at == 0, hi, jnp.where(at == 1, mid, jnp.where(at == 2, low, zero))).astype(BF)


def step_of(ns):
    return 256 if ns % 256 == 0 else ns


def turn(block, by):
    return jnp.concatenate([block[:, by:], block[:, :by]], axis=1)


def fold(rows):
    return jnp.sum(rows, axis=0, keepdims=True)


def vmem(n):
    return [pl.BlockSpec(memory_space=pltpu.VMEM)] * n


def pack_kernel(parts, pairs, bs, chunk, table, s_ref, tm_ref, *refs):
    vals, gains = refs[:parts], refs[parts : 2 * parts]
    refs = refs[2 * parts :]
    if table:
        source_ref, cols_ref = refs[:2]
        refs = refs[2:]
        tables = refs[parts:]
        for d in range(parts):
            tables[d][...] = jnp.zeros(tables[d].shape, F32)
            begin = pl.multiple_of((s_ref[0] ^ d) * chunk, chunk)
            tables[d][:chunk, :] = source_ref[pl.ds(begin, chunk), :]
            for e in range(cols_ref.shape[0]):
                for i in range(cols_ref.shape[1]):
                    at = chunk + e * cols_ref.shape[1] + i
                    line = cols_ref[e, i : i + 1, :].astype(F32)
                    tables[d][at : at + 1, : line.shape[1]] = line
    outs = refs[:parts]
    for d in range(parts):
        for q in range(pairs):
            for i in range(2):
                outs[d][0, q, i * bs : (i + 1) * bs, :] = vals[d][0, 2 * q + i, :, : 2 * bs]
            base = 2 * bs
            third = jnp.concatenate(
                [vals[d][0, 2 * q, :, 2 * bs :], vals[d][0, 2 * q + 1, :, 2 * bs :]], axis=1
            )
            outs[d][0, q, base : base + bs, :] = third
            base = 3 * bs
            outs[d][0, q, base : base + 2 * bs, :] = gains[d][0, q * 2 * bs : (q + 1) * 2 * bs, :]


def pack(position, span, dyn_vals, gain, parts, chunk, first, count, table=()):
    _, lb, bs, width = dyn_vals.shape
    rows, obs = gain.shape[1:]
    pairs = lb // 2

    def from_part(d, trail):
        return lambda j, s, t: ((s[0] ^ d) * chunk + first + j,) + (0,) * trail

    shape = (count, pairs, 5 * bs, 2 * bs)
    tables = [jax.ShapeDtypeStruct((chunk + 3 * lb, lb * bs), F32)] * (parts if table else 0)
    return pl.pallas_call(
        functools.partial(pack_kernel, parts, pairs, bs, chunk, bool(table)),
        grid_spec=pltpu.PrefetchScalarGridSpec(
            num_scalar_prefetch=2,
            grid=(count,),
            in_specs=[pl.BlockSpec((1, lb, bs, width), from_part(d, 3)) for d in range(parts)]
            + [pl.BlockSpec((1, rows, obs), from_part(d, 2)) for d in range(parts)]
            + vmem(len(table)),
            out_specs=[pl.BlockSpec((1,) + shape[1:], lambda j, s, t: (j, 0, 0, 0))] * parts
            + vmem(len(tables)),
        ),
        out_shape=[jax.ShapeDtypeStruct(shape, BF)] * parts + tables,
        compiler_params=pltpu.CompilerParams(vmem_limit_bytes=VMEM_LIMIT),
    )(position, span, *([dyn_vals] * parts), *([gain] * parts), *table)


def plan_kernel(parts, chunk, *refs):
    small, blocks, counts, out_ref = refs[:parts], refs[parts], refs[parts + 1], refs[parts + 2]
    steps = counts.shape[1]
    each = small[0].shape[0] - chunk
    for d in range(parts):
        out_ref[d * each : (d + 1) * each, :] = small[d][chunk:, :steps].astype(jnp.int32)
    out_ref[parts * each : parts * each + 2, :] = blocks[...]
    out_ref[parts * each + 2 : parts * each + 3, :] = counts[...]


def plan_of(small, blocks, counts, chunk):
    parts = len(small)
    each = small[0].shape[0] - chunk
    return pl.pallas_call(
        functools.partial(plan_kernel, parts, chunk),
        in_specs=vmem(parts + 2),
        out_specs=vmem(1)[0],
        out_shape=jax.ShapeDtypeStruct((parts * each + 3, counts.shape[1]), jnp.int32),
        compiler_params=pltpu.CompilerParams(vmem_limit_bytes=VMEM_LIMIT),
        name="plan",
    )(*small, blocks, counts)


def chunk_kernel(
    parts, pairs, bs, chunk, first, count, s_ref, tm_ref, plan_ref, *refs
):
    each = 6 * pairs
    data, small = refs[:parts], refs[parts : 2 * parts]
    op_ref, values_ref, prior_ref, before, vec_in = refs[2 * parts : 2 * parts + 5]
    maps, vec_ref = refs[2 * parts + 5 : 2 * parts + 7]
    dyn, gains, source, chosen, elements, offsets = refs[2 * parts + 7 :]
    s = s_ref[0]
    ns = parts * pairs * 2 * bs
    map_in = before.at[before.shape[0] - 1]
    lane = lax.broadcasted_iota(jnp.int32, (bs, 2 * bs), 1)
    left = lane < bs
    zero = jnp.zeros((), BF)
    tiles = parts * pairs
    lane_row = lax.broadcasted_iota(jnp.int32, (1, 2 * bs), 1)
    slot = lax.broadcasted_iota(jnp.int32, (2 * bs, 1), 0)
    for d in range(parts):
        for q in range(pairs):
            source[(s ^ d) * pairs + q] = small[d][:chunk, q * 2 * bs : (q + 1) * 2 * bs]
    for j in range(count):
        here = first + j
        k = s * chunk + here
        dyn[...] = jnp.zeros(dyn.shape, BF)
        for d in range(parts):
            for q in range(pairs):
                group = (s ^ d) * pairs + q
                gains[pl.ds(pl.multiple_of(group * 2 * bs, 2 * bs), 2 * bs), :] = data[d][
                    j, q, 3 * bs : 5 * bs, :
                ]
                third = data[d][j, q, 2 * bs : 3 * bs, :]
                third_turned = turn(third, bs)
                for i in range(2):
                    both = data[d][j, q, i * bs : (i + 1) * bs, :]
                    both_turned = turn(both, bs)
                    lefts = (both, both_turned, third if i == 0 else third_turned)
                    rights = (both_turned, both, third_turned if i == 0 else third)
                    row = pl.multiple_of(group * 2 * bs + i * bs, bs)
                    placed = [jnp.where(left, both, zero) if i == 0 else jnp.where(left, zero, both_turned)]
                    at = [group]
                    for e in range(1, 3):
                        column = plan_ref[d * each + e * 2 * pairs + 2 * q + i, k]
                        at.append(column >> 1)
                        placed.append(
                            jnp.where(
                                (column & 1) == 0,
                                jnp.where(left, lefts[e], zero),
                                jnp.where(left, zero, rights[e]),
                            )
                        )
                    for e in range(3):
                        value = placed[e]
                        for f in range(3):
                            if f != e:
                                value = value + jnp.where(at[e] == at[f], placed[f], zero)
                        dyn[at[e], pl.ds(row, bs), :] = value
        operator = op_ref[k].astype(F32)
        diagonal = jnp.concatenate(
            [jnp.where(left, operator, 0.0), jnp.where(left, 0.0, operator)], axis=0
        ).astype(BF)
        picks = []
        for o in range(2):
            block = plan_ref[parts * each + o, k]
            for tile in range(tiles):
                found = pl.ds(pl.multiple_of(block * bs, bs), bs)
                chosen[o * bs : (o + 1) * bs, tile * 2 * bs : (tile + 1) * 2 * bs] = (
                    dyn[tile, found, :]
                )
            row = source[block >> 1, pl.ds(here, 1), :]
            turned = pltpu.roll(row, bs, 1)
            picks.append(jnp.where((block & 1) == o, row, turned))
        image = tn(diagonal, chosen[...])
        masked = jnp.where(slot < plan_ref[parts * each + 2, k], image, 0.0).astype(BF)
        pick = jnp.where(lane_row < bs, picks[0], picks[1])
        source_image = fold(nn(split3(pick), diagonal)).astype(BF).astype(F32)
        innovation = jnp.where(
            lane_row < plan_ref[parts * each + 2, k], values_ref[pl.ds(k, 1), :] - source_image, 0.0
        )
        shift = fold(nt(split3(innovation), gains[...]))
        shift = shift + jnp.concatenate(
            [source[g, pl.ds(here, 1), :] for g in range(parts * pairs)], axis=1
        )
        offsets[j : j + 1, :] = shift
        for g in range(parts * pairs):
            rows = slice(g * 2 * bs, (g + 1) * 2 * bs)
            correction = nn(gains[rows, :], masked)
            for tile in range(tiles):
                lanes = slice(tile * 2 * bs, (tile + 1) * 2 * bs)
                forward = dyn[tile, rows, :].astype(F32)
                elements[j, rows, lanes] = (forward - correction[:, lanes]).astype(BF)
    if first == 0:
        begin = jnp.logical_and(s == 0, tm_ref[0] == 0)
        vec = jnp.where(begin, prior_ref[...], 0.0)
    else:
        vec = vec_in[...]
    for j in range(count):
        element = elements[j]
        vec = fold(nt(split3(vec), element)) + offsets[j : j + 1, :]
        held = map_in if j == 0 else maps.at[j - 1]
        target = maps.at[j]
        for r in range(0, ns, step_of(ns)):
            rows, below = slice(r, r + step_of(ns)), slice(ns + r, ns + r + step_of(ns))
            if first == 0 and j == 0:
                across = lax.broadcasted_iota(jnp.int32, (step_of(ns), ns), 1)
                down = lax.broadcasted_iota(jnp.int32, (step_of(ns), ns), 0) + r
                unit = jnp.where(across == down, 1.0, 0.0).astype(BF)
                target[rows, :] = nt(unit, element).astype(BF)
                target[below, :] = jnp.zeros((step_of(ns), ns), BF)
                continue
            moved = nt(held[rows, :], element)
            if first > 0 or j > 1:
                moved = moved + nt(held[below, :], element)
            top = moved.astype(BF)
            target[rows, :] = top
            target[below, :] = (moved - top.astype(F32)).astype(BF)
        target[2 * ns :, :] = split3(vec)
    vec_ref[...] = vec


def chunk_piece(
    position, span, plan, data, small, obs_op, obs_values, prior, state, chunk, first, count
):
    parts = len(data)
    pairs, _, width = data[0].shape[1:]
    bs = width // 2
    ns = parts * pairs * width
    if state is None:
        state = (data[0], prior)
    return pl.pallas_call(
        functools.partial(chunk_kernel, parts, pairs, bs, chunk, first, count),
        grid_spec=pltpu.PrefetchScalarGridSpec(
            num_scalar_prefetch=3,
            grid=(),
            in_specs=vmem(2 * parts + 5),
            out_specs=vmem(2),
            scratch_shapes=[
                pltpu.VMEM((parts * pairs, ns, width), BF),
                pltpu.VMEM((ns, width), BF),
                pltpu.VMEM((parts * pairs, chunk, width), F32),
                pltpu.VMEM((width, ns), BF),
                pltpu.VMEM((count, ns, ns), BF),
                pltpu.VMEM((8, ns), F32),
            ],
        ),
        out_shape=[
            jax.ShapeDtypeStruct((count, 2 * ns + ROWS, ns), BF),
            jax.ShapeDtypeStruct((1, ns), F32),
        ],
        compiler_params=pltpu.CompilerParams(vmem_limit_bytes=VMEM_LIMIT),
    )(
        position, span, plan, *data, *small, obs_op, obs_values, prior, *state,
    )


def apply_map(row, held):
    ns = held.shape[1]
    parts = split3(row)
    moved = fold(nn(parts, held[:ns, :]) + nn(parts, held[ns : 2 * ns, :]))
    return moved + fold(held[2 * ns :, :].astype(F32))


def join_kernel(one, two, out_ref):
    ns = one.shape[1]
    for r in range(0, ns, step_of(ns)):
        rows, below = slice(r, r + step_of(ns)), slice(ns + r, ns + r + step_of(ns))
        product = nn(one[rows, :], two[:ns, :]) + (
            nn(one[rows, :], two[ns : 2 * ns, :]) + nn(one[below, :], two[:ns, :])
        )
        top = product.astype(BF)
        out_ref[rows, :] = top
        out_ref[below, :] = (product - top.astype(F32)).astype(BF)
    out_ref[2 * ns :, :] = split3(apply_map(fold(one[2 * ns :, :].astype(F32)), two))


def join(one, two):
    return pl.pallas_call(
        join_kernel,
        in_specs=vmem(2),
        out_specs=vmem(1)[0],
        out_shape=jax.ShapeDtypeStruct(two.shape, BF),
        compiler_params=pltpu.CompilerParams(vmem_limit_bytes=VMEM_LIMIT),
        name="join",
    )(one, two)


def hop_kernel(row_ref, *refs):
    current = row_ref[...]
    for held in refs[:-1]:
        current = apply_map(current, held)
    refs[-1][...] = current


def hop(row, *maps):
    return pl.pallas_call(
        hop_kernel,
        in_specs=vmem(1 + len(maps)),
        out_specs=vmem(1)[0],
        out_shape=jax.ShapeDtypeStruct(row.shape, F32),
        compiler_params=pltpu.CompilerParams(vmem_limit_bytes=VMEM_LIMIT),
        name="hop",
    )(row, *maps)


def span_kernel(leaders, s_ref, row_ref, *refs):
    maps, out_ref = refs[:leaders], refs[leaders]
    for mine in range(leaders):

        @pl.when(s_ref[0] // 2 == mine)
        def _():
            current = row_ref[...]
            for p in range(leaders):
                current = apply_map(current, maps[p ^ mine])
            out_ref[...] = current


def span_hop(position, row, maps):
    leaders = len(maps)
    return pl.pallas_call(
        functools.partial(span_kernel, leaders),
        grid_spec=pltpu.PrefetchScalarGridSpec(
            num_scalar_prefetch=1,
            grid=(),
            in_specs=vmem(1 + leaders),
            out_specs=vmem(1)[0],
        ),
        out_shape=jax.ShapeDtypeStruct(row.shape, F32),
        compiler_params=pltpu.CompilerParams(vmem_limit_bytes=VMEM_LIMIT),
        name="span_hop",
    )(position, row, *maps)


def span_join_kernel(s_ref, own, far, out_ref):
    @pl.when(s_ref[0] // 2 == 0)
    def _():
        join_kernel(own, far, out_ref)

    @pl.when(s_ref[0] // 2 == 1)
    def _():
        join_kernel(far, own, out_ref)


def span_join(position, own, far):
    return pl.pallas_call(
        span_join_kernel,
        grid_spec=pltpu.PrefetchScalarGridSpec(
            num_scalar_prefetch=1, grid=(), in_specs=vmem(2), out_specs=vmem(1)[0]
        ),
        out_shape=jax.ShapeDtypeStruct(own.shape, BF),
        compiler_params=pltpu.CompilerParams(vmem_limit_bytes=VMEM_LIMIT),
        name="span_join",
    )(position, own, far)


def lead_kernel(leaders, early, s_ref, tm_ref, row_ref, direct_ref, *refs):
    sets, out_ref = (refs[:leaders], refs[leaders : 2 * leaders]), refs[2 * leaders]

    @pl.when(tm_ref[0] < early)
    def _():
        out_ref[...] = direct_ref[...]

    for mine in range(leaders):
        for late in range(2):
            reached = (tm_ref[0] > early) if late else (tm_ref[0] == early)

            @pl.when(jnp.logical_and(s_ref[0] // 2 == mine, reached))
            def _():
                current = row_ref[...]
                for p in range(mine):
                    current = apply_map(current, sets[late][p ^ mine])
                out_ref[...] = current


def lead(position, span, row, direct, maps, maps_late, early):
    leaders = len(maps)
    return pl.pallas_call(
        functools.partial(lead_kernel, leaders, early),
        grid_spec=pltpu.PrefetchScalarGridSpec(
            num_scalar_prefetch=2,
            grid=(),
            in_specs=vmem(2 + 2 * leaders),
            out_specs=vmem(1)[0],
        ),
        out_shape=jax.ShapeDtypeStruct(row.shape, F32),
        compiler_params=pltpu.CompilerParams(vmem_limit_bytes=VMEM_LIMIT),
        name="lead",
    )(position, span, row, direct, *maps, *maps_late)


def sweep_kernel(pieces, parts, s_ref, tm_ref, *refs):
    own_ref, told_ref, first_map, first_vec, map_ref = refs[:5]
    stages, outs = refs[5 : 5 + pieces], refs[5 + pieces : 5 + pieces + parts]
    current_ref, spread = refs[5 + pieces + parts :]
    s = s_ref[0]

    @pl.when(s % 2 == 0)
    def _():
        current_ref[...] = told_ref[...]

    @pl.when(jnp.logical_and(s % 2 == 1, tm_ref[0] == 0))
    def _():
        current_ref[...] = apply_map(own_ref[...], first_map) + first_vec[...]

    @pl.when(jnp.logical_and(s % 2 == 1, tm_ref[0] > 0))
    def _():
        current_ref[...] = apply_map(own_ref[...], map_ref)

    entry = current_ref[...]
    at = 0
    width = spread.shape[2]
    for p in range(pieces):
        for j in range(stages[p].shape[0]):
            mean = apply_map(entry, stages[p].at[j])
            for d in range(parts):
                spread[d, at : at + 1, :] = mean[:, d * width : (d + 1) * width]
            at += 1
    for d in range(parts):
        outs[d][...] = spread[s ^ d]


def sweep(position, span, own, told, even, stages, parts):
    ns = own.shape[1]
    pieces = len(stages)
    chunk = sum(x.shape[0] for x in stages)
    width = ns // parts
    return pl.pallas_call(
        functools.partial(sweep_kernel, pieces, parts),
        grid_spec=pltpu.PrefetchScalarGridSpec(
            num_scalar_prefetch=2,
            grid=(),
            in_specs=vmem(5 + pieces),
            out_specs=vmem(parts),
            scratch_shapes=[
                pltpu.VMEM((1, ns), F32),
                pltpu.VMEM((parts, chunk, width), F32),
            ],
        ),
        out_shape=[jax.ShapeDtypeStruct((chunk, width), F32)] * parts,
        compiler_params=pltpu.CompilerParams(vmem_limit_bytes=VMEM_LIMIT),
        name="sweep",
    )(position, span, own, told, *even, *stages)


def gather_kernel(parts, s_ref, *refs):
    blocks, out_ref = refs[:parts], refs[parts]
    rows = blocks[0].shape[0]
    for d in range(parts):
        out_ref[pl.ds(pl.multiple_of((s_ref[0] ^ d) * rows, rows), rows), :] = blocks[d][...]


def gather(position, blocks):
    rows, width = blocks[0].shape
    parts = len(blocks)
    return pl.pallas_call(
        functools.partial(gather_kernel, parts),
        grid_spec=pltpu.PrefetchScalarGridSpec(
            num_scalar_prefetch=1, grid=(), in_specs=vmem(parts), out_specs=vmem(1)[0]
        ),
        out_shape=jax.ShapeDtypeStruct((parts * rows, width), F32),
        compiler_params=pltpu.CompilerParams(vmem_limit_bytes=VMEM_LIMIT),
        name="gather",
    )(position, *blocks)


PIECES = 5


def piece_sizes(chunk):
    base, more = divmod(chunk - 2, PIECES - 2)
    return [base + 1] * more + [base] * (PIECES - 2 - more) + [1, 1]


def means(dyn_cols, dyn_vals, obs_blocks, obs_op, obs_counts, obs_values, gain, sources, prior):
    steps, _, _, _ = dyn_vals.shape
    parts = lax.axis_size("state")
    spans = lax.axis_size("tm")
    chunk = steps // parts
    ns = prior.shape[0]
    s = lax.axis_index("state")
    t = lax.axis_index("tm")
    position = s.reshape(1).astype(jnp.int32)
    span = t.reshape(1).astype(jnp.int32)
    prior_row = prior.reshape(1, ns)

    def across(x, d):
        return lax.ppermute(x, "state", [(i, i ^ d) for i in range(parts)])

    def send(x, pairs):
        return lax.ppermute(x, ("tm", "state"), [(a * parts + b, c * parts + e) for (a, b), (c, e) in pairs])

    order = sorted(range(1, parts), reverse=True)
    sizes = piece_sizes(chunk)
    firsts = [sum(sizes[:n]) for n in range(len(sizes))]
    vals_far = pltpu.with_memory_space_constraint(dyn_vals, pltpu.HBM)
    gain_far = pltpu.with_memory_space_constraint(gain, pltpu.HBM)
    pieces = []
    for n, (first, size) in enumerate(zip(firsts, sizes)):
        source_arrays = (vals_far, gain_far) if n == 0 else (dyn_vals, gain)
        table = (sources, dyn_cols.transpose(2, 1, 0)) if n == 1 else ()
        packed = pack(position, span, *source_arrays, parts, chunk, first, size, table)
        arrived = {0: packed[0]}
        for d in order:
            arrived[d] = across(packed[d], d)
        pieces.append([arrived[d] for d in range(parts)])
        if n == 1:
            small = {0: packed[parts]}
            for d in order:
                small[d] = across(packed[parts + d], d)
            small = [small[d] for d in range(parts)]

    plan = plan_of(small, obs_blocks.T, obs_counts.reshape(1, steps), chunk)
    state = None
    stages = []
    for first, size, data in zip(firsts, sizes, pieces):
        state = chunk_piece(
            position, span, plan, data, small, obs_op, obs_values, prior_row, state, chunk, first, size
        )
        stages.append(state[0])
    vec = state[1]
    chunk_map = state[0].reshape(state[0].shape[1:])

    leads = [2 * p + 1 for p in range(parts // 2)]
    to_lead = [((a, l - 1), (a, l)) for a in range(spans) for l in leads]
    map_even = send(chunk_map, [pair for pair in to_lead if pair[0][0] > 0])
    first_vec = send(vec, to_lead[:1])
    first_map = send(chunk_map, to_lead[1 : len(leads)])
    current = hop(first_vec, chunk_map)
    pair = join(map_even, chunk_map)

    early = min(2, spans - 1)
    maps, maps_late = [pair], [pair]
    for d in range(2, parts, 2):
        pairs = [((a, l), (a, l ^ d)) for a in range(early, spans) for l in leads]
        maps.append(send(pair, pairs[: len(leads)]))
        maps_late.append(send(pair, pairs[len(leads) :]))

    direct = jnp.zeros((1, ns), F32)
    entry = jnp.zeros((1, ns), F32)
    for g in range(early):
        held = (pair,) if g > 0 else (first_map, chunk_map)
        for p in range(1, len(leads)):
            arriving = send(current, [((g, leads[p - 1]), (g, leads[p]))])
            direct = direct + arriving
            current = hop(arriving, *held)
        if g + 1 < early:
            arriving = send(current, [((g, leads[-1]), (g + 1, leads[0]))])
            direct = direct + arriving
            current = hop(arriving, pair)
        else:
            for l in leads:
                entry = entry + send(current, [((g, leads[-1]), (g + 1, l))])

    arriving = entry
    joined = span_join(position, *maps_late) if len(leads) == 2 else None
    for h in range(early, spans - 1):
        if h < early + 2 or joined is None:
            current = span_hop(position, arriving, maps if h == early else maps_late)
        else:
            current = hop(arriving, joined)
        arriving = send(current, [((h, l), (h + 1, l)) for l in leads])
        entry = entry + arriving

    own = lead(position, span, entry, direct, maps, maps_late, early)
    told = send(own, [(b, a) for a, b in to_lead])
    mine = sweep(
        position, span, own, told, (first_map, first_vec, map_even), stages, parts
    )
    got = {0: mine[0]}
    for d in order:
        got[d] = across(mine[d], d)
    return gather(position, [got[d] for d in range(parts)])


def solution(mesh):
    return jax.shard_map(
        means,
        mesh=mesh,
        in_specs=(
            P("tm", "state", None),
            P("tm", "state", None, None),
            P("tm", None),
            P("tm", None, None),
            P("tm"),
            P("tm", None),
            P("tm", "state", None),
            P("tm", "state"),
            P(),
        ),
        out_specs=P("tm", "state"),
        check_vma=False,
    )
```

```python
import functools

import jax
import jax.numpy as jnp
from jax import lax
from jax.experimental import pallas as pl
from jax.experimental.pallas import tpu as pltpu
from jax.sharding import PartitionSpec as P


BF = jnp.bfloat16
F32 = jnp.float32
VMEM_LIMIT = 12 * 1024 * 1024
ROWS = 16


def nt(a, b):
    return lax.dot_general(a, b, (((1,), (1,)), ((), ())), preferred_element_type=F32)


def nn(a, b):
    return lax.dot_general(a, b, (((1,), (0,)), ((), ())), preferred_element_type=F32)


def tn(a, b):
    return lax.dot_general(a, b, (((0,), (0,)), ((), ())), preferred_element_type=F32)


def split3(row):
    hi = row.astype(BF).astype(F32)
    rest = row - hi
    mid = rest.astype(BF).astype(F32)
    low = rest - mid
    at = lax.broadcasted_iota(jnp.int32, (ROWS, row.shape[1]), 0)
    zero = jnp.zeros((), F32)
    return jnp.where(at == 0, hi, jnp.where(at == 1, mid, jnp.where(at == 2, low, zero))).astype(BF)


def step_of(ns):
    return 256 if ns % 256 == 0 else ns


def turn(block, by):
    return jnp.concatenate([block[:, by:], block[:, :by]], axis=1)


def fold(rows):
    return jnp.sum(rows, axis=0, keepdims=True)


def vmem(n):
    return [pl.BlockSpec(memory_space=pltpu.VMEM)] * n


def pack_kernel(parts, pairs, bs, chunk, table, s_ref, tm_ref, *refs):
    vals, gains = refs[:parts], refs[parts : 2 * parts]
    refs = refs[2 * parts :]
    if table:
        source_ref, cols_ref = refs[:2]
        refs = refs[2:]
        tables = refs[parts:]
        for d in range(parts):
            tables[d][...] = jnp.zeros(tables[d].shape, F32)
            begin = pl.multiple_of((s_ref[0] ^ d) * chunk, chunk)
            tables[d][:chunk, :] = source_ref[pl.ds(begin, chunk), :]
            for e in range(cols_ref.shape[0]):
                for i in range(cols_ref.shape[1]):
                    at = chunk + e * cols_ref.shape[1] + i
                    line = cols_ref[e, i : i + 1, :].astype(F32)
                    tables[d][at : at + 1, : line.shape[1]] = line
    outs = refs[:parts]
    for d in range(parts):
        for q in range(pairs):
            for i in range(2):
                outs[d][0, q, i * bs : (i + 1) * bs, :] = vals[d][0, 2 * q + i, :, : 2 * bs]
            base = 2 * bs
            third = jnp.concatenate(
                [vals[d][0, 2 * q, :, 2 * bs :], vals[d][0, 2 * q + 1, :, 2 * bs :]], axis=1
            )
            outs[d][0, q, base : base + bs, :] = third
            base = 3 * bs
            outs[d][0, q, base : base + 2 * bs, :] = gains[d][0, q * 2 * bs : (q + 1) * 2 * bs, :]


def pack(position, span, dyn_vals, gain, parts, chunk, first, count, table=()):
    _, lb, bs, width = dyn_vals.shape
    rows, obs = gain.shape[1:]
    pairs = lb // 2

    def from_part(d, trail):
        return lambda j, s, t: ((s[0] ^ d) * chunk + first + j,) + (0,) * trail

    shape = (count, pairs, 5 * bs, 2 * bs)
    tables = [jax.ShapeDtypeStruct((chunk + 3 * lb, lb * bs), F32)] * (parts if table else 0)
    return pl.pallas_call(
        functools.partial(pack_kernel, parts, pairs, bs, chunk, bool(table)),
        grid_spec=pltpu.PrefetchScalarGridSpec(
            num_scalar_prefetch=2,
            grid=(count,),
            in_specs=[pl.BlockSpec((1, lb, bs, width), from_part(d, 3)) for d in range(parts)]
            + [pl.BlockSpec((1, rows, obs), from_part(d, 2)) for d in range(parts)]
            + vmem(len(table)),
            out_specs=[pl.BlockSpec((1,) + shape[1:], lambda j, s, t: (j, 0, 0, 0))] * parts
            + vmem(len(tables)),
        ),
        out_shape=[jax.ShapeDtypeStruct(shape, BF)] * parts + tables,
        compiler_params=pltpu.CompilerParams(vmem_limit_bytes=VMEM_LIMIT),
    )(position, span, *([dyn_vals] * parts), *([gain] * parts), *table)


def plan_kernel(parts, chunk, *refs):
    small, blocks, counts, out_ref = refs[:parts], refs[parts], refs[parts + 1], refs[parts + 2]
    steps = counts.shape[1]
    each = small[0].shape[0] - chunk
    for d in range(parts):
        out_ref[d * each : (d + 1) * each, :] = small[d][chunk:, :steps].astype(jnp.int32)
    out_ref[parts * each : parts * each + 2, :] = blocks[...]
    out_ref[parts * each + 2 : parts * each + 3, :] = counts[...]


def plan_of(small, blocks, counts, chunk):
    parts = len(small)
    each = small[0].shape[0] - chunk
    return pl.pallas_call(
        functools.partial(plan_kernel, parts, chunk),
        in_specs=vmem(parts + 2),
        out_specs=vmem(1)[0],
        out_shape=jax.ShapeDtypeStruct((parts * each + 3, counts.shape[1]), jnp.int32),
        compiler_params=pltpu.CompilerParams(vmem_limit_bytes=VMEM_LIMIT),
        name="plan",
    )(*small, blocks, counts)


def chunk_kernel(
    parts, pairs, bs, chunk, first, count, s_ref, tm_ref, plan_ref, *refs
):
    each = 6 * pairs
    data, small = refs[:parts], refs[parts : 2 * parts]
    op_ref, values_ref, prior_ref, before, vec_in = refs[2 * parts : 2 * parts + 5]
    maps, vec_ref = refs[2 * parts + 5 : 2 * parts + 7]
    dyn, gains, source, chosen, elements, offsets = refs[2 * parts + 7 :]
    s = s_ref[0]
    ns = parts * pairs * 2 * bs
    map_in = before.at[before.shape[0] - 1]
    lane = lax.broadcasted_iota(jnp.int32, (bs, 2 * bs), 1)
    left = lane < bs
    zero = jnp.zeros((), BF)
    tiles = parts * pairs
    lane_row = lax.broadcasted_iota(jnp.int32, (1, 2 * bs), 1)
    slot = lax.broadcasted_iota(jnp.int32, (2 * bs, 1), 0)
    for d in range(parts):
        for q in range(pairs):
            source[(s ^ d) * pairs + q] = small[d][:chunk, q * 2 * bs : (q + 1) * 2 * bs]
    for j in range(count):
        here = first + j
        k = s * chunk + here
        dyn[...] = jnp.zeros(dyn.shape, BF)
        for d in range(parts):
            for q in range(pairs):
                group = (s ^ d) * pairs + q
                gains[pl.ds(pl.multiple_of(group * 2 * bs, 2 * bs), 2 * bs), :] = data[d][
                    j, q, 3 * bs : 5 * bs, :
                ]
                third = data[d][j, q, 2 * bs : 3 * bs, :]
                third_turned = turn(third, bs)
                for i in range(2):
                    both = data[d][j, q, i * bs : (i + 1) * bs, :]
                    both_turned = turn(both, bs)
                    lefts = (both, both_turned, third if i == 0 else third_turned)
                    rights = (both_turned, both, third_turned if i == 0 else third)
                    row = pl.multiple_of(group * 2 * bs + i * bs, bs)
                    placed = [jnp.where(left, both, zero) if i == 0 else jnp.where(left, zero, both_turned)]
                    at = [group]
                    for e in range(1, 3):
                        column = plan_ref[d * each + e * 2 * pairs + 2 * q + i, k]
                        at.append(column >> 1)
                        placed.append(
                            jnp.where(
                                (column & 1) == 0,
                                jnp.where(left, lefts[e], zero),
                                jnp.where(left, zero, rights[e]),
                            )
                        )
                    for e in range(3):
                        value = placed[e]
                        for f in range(3):
                            if f != e:
                                value = value + jnp.where(at[e] == at[f], placed[f], zero)
                        dyn[at[e], pl.ds(row, bs), :] = value
        operator = op_ref[k].astype(F32)
        diagonal = jnp.concatenate(
            [jnp.where(left, operator, 0.0), jnp.where(left, 0.0, operator)], axis=0
        ).astype(BF)
        picks = []
        for o in range(2):
            block = plan_ref[parts * each + o, k]
            for tile in range(tiles):
                found = pl.ds(pl.multiple_of(block * bs, bs), bs)
                chosen[o * bs : (o + 1) * bs, tile * 2 * bs : (tile + 1) * 2 * bs] = (
                    dyn[tile, found, :]
                )
            row = source[block >> 1, pl.ds(here, 1), :]
            turned = pltpu.roll(row, bs, 1)
            picks.append(jnp.where((block & 1) == o, row, turned))
        image = tn(diagonal, chosen[...])
        masked = jnp.where(slot < plan_ref[parts * each + 2, k], image, 0.0).astype(BF)
        pick = jnp.where(lane_row < bs, picks[0], picks[1])
        source_image = fold(nn(split3(pick), diagonal)).astype(BF).astype(F32)
        innovation = jnp.where(
            lane_row < plan_ref[parts * each + 2, k], values_ref[pl.ds(k, 1), :] - source_image, 0.0
        )
        shift = fold(nt(split3(innovation), gains[...]))
        shift = shift + jnp.concatenate(
            [source[g, pl.ds(here, 1), :] for g in range(parts * pairs)], axis=1
        )
        offsets[j : j + 1, :] = shift
        for g in range(parts * pairs):
            rows = slice(g * 2 * bs, (g + 1) * 2 * bs)
            correction = nn(gains[rows, :], masked)
            for tile in range(tiles):
                lanes = slice(tile * 2 * bs, (tile + 1) * 2 * bs)
                forward = dyn[tile, rows, :].astype(F32)
                elements[j, rows, lanes] = (forward - correction[:, lanes]).astype(BF)
    if first == 0:
        begin = jnp.logical_and(s == 0, tm_ref[0] == 0)
        vec = jnp.where(begin, prior_ref[...], 0.0)
    else:
        vec = vec_in[...]
    for j in range(count):
        element = elements[j]
        vec = fold(nt(split3(vec), element)) + offsets[j : j + 1, :]
        held = map_in if j == 0 else maps.at[j - 1]
        target = maps.at[j]
        for r in range(0, ns, step_of(ns)):
            rows, below = slice(r, r + step_of(ns)), slice(ns + r, ns + r + step_of(ns))
            if first == 0 and j == 0:
                across = lax.broadcasted_iota(jnp.int32, (step_of(ns), ns), 1)
                down = lax.broadcasted_iota(jnp.int32, (step_of(ns), ns), 0) + r
                unit = jnp.where(across == down, 1.0, 0.0).astype(BF)
                target[rows, :] = nt(unit, element).astype(BF)
                target[below, :] = jnp.zeros((step_of(ns), ns), BF)
                continue
            moved = nt(held[rows, :], element)
            if first > 0 or j > 1:
                moved = moved + nt(held[below, :], element)
            top = moved.astype(BF)
            target[rows, :] = top
            target[below, :] = (moved - top.astype(F32)).astype(BF)
        target[2 * ns :, :] = split3(vec)
    vec_ref[...] = vec


def chunk_piece(
    position, span, plan, data, small, obs_op, obs_values, prior, state, chunk, first, count
):
    parts = len(data)
    pairs, _, width = data[0].shape[1:]
    bs = width // 2
    ns = parts * pairs * width
    if state is None:
        state = (data[0], prior)
    return pl.pallas_call(
        functools.partial(chunk_kernel, parts, pairs, bs, chunk, first, count),
        grid_spec=pltpu.PrefetchScalarGridSpec(
            num_scalar_prefetch=3,
            grid=(),
            in_specs=vmem(2 * parts + 5),
            out_specs=vmem(2),
            scratch_shapes=[
                pltpu.VMEM((parts * pairs, ns, width), BF),
                pltpu.VMEM((ns, width), BF),
                pltpu.VMEM((parts * pairs, chunk, width), F32),
                pltpu.VMEM((width, ns), BF),
                pltpu.VMEM((count, ns, ns), BF),
                pltpu.VMEM((8, ns), F32),
            ],
        ),
        out_shape=[
            jax.ShapeDtypeStruct((count, 2 * ns + ROWS, ns), BF),
            jax.ShapeDtypeStruct((1, ns), F32),
        ],
        compiler_params=pltpu.CompilerParams(vmem_limit_bytes=VMEM_LIMIT),
    )(
        position, span, plan, *data, *small, obs_op, obs_values, prior, *state,
    )


def apply_map(row, held):
    ns = held.shape[1]
    parts = split3(row)
    moved = fold(nn(parts, held[:ns, :]) + nn(parts, held[ns : 2 * ns, :]))
    return moved + fold(held[2 * ns :, :].astype(F32))


def join_kernel(one, two, out_ref):
    ns = one.shape[1]
    for r in range(0, ns, step_of(ns)):
        rows, below = slice(r, r + step_of(ns)), slice(ns + r, ns + r + step_of(ns))
        product = nn(one[rows, :], two[:ns, :]) + (
            nn(one[rows, :], two[ns : 2 * ns, :]) + nn(one[below, :], two[:ns, :])
        )
        top = product.astype(BF)
        out_ref[rows, :] = top
        out_ref[below, :] = (product - top.astype(F32)).astype(BF)
    out_ref[2 * ns :, :] = split3(apply_map(fold(one[2 * ns :, :].astype(F32)), two))


def join(one, two):
    return pl.pallas_call(
        join_kernel,
        in_specs=vmem(2),
        out_specs=vmem(1)[0],
        out_shape=jax.ShapeDtypeStruct(two.shape, BF),
        compiler_params=pltpu.CompilerParams(vmem_limit_bytes=VMEM_LIMIT),
        name="join",
    )(one, two)


def hop_kernel(row_ref, *refs):
    current = row_ref[...]
    for held in refs[:-1]:
        current = apply_map(current, held)
    refs[-1][...] = current


def hop(row, *maps):
    return pl.pallas_call(
        hop_kernel,
        in_specs=vmem(1 + len(maps)),
        out_specs=vmem(1)[0],
        out_shape=jax.ShapeDtypeStruct(row.shape, F32),
        compiler_params=pltpu.CompilerParams(vmem_limit_bytes=VMEM_LIMIT),
        name="hop",
    )(row, *maps)


def span_kernel(leaders, s_ref, row_ref, *refs):
    maps, out_ref = refs[:leaders], refs[leaders]
    for mine in range(leaders):

        @pl.when(s_ref[0] // 2 == mine)
        def _():
            current = row_ref[...]
            for p in range(leaders):
                current = apply_map(current, maps[p ^ mine])
            out_ref[...] = current


def span_hop(position, row, maps):
    leaders = len(maps)
    return pl.pallas_call(
        functools.partial(span_kernel, leaders),
        grid_spec=pltpu.PrefetchScalarGridSpec(
            num_scalar_prefetch=1,
            grid=(),
            in_specs=vmem(1 + leaders),
            out_specs=vmem(1)[0],
        ),
        out_shape=jax.ShapeDtypeStruct(row.shape, F32),
        compiler_params=pltpu.CompilerParams(vmem_limit_bytes=VMEM_LIMIT),
        name="span_hop",
    )(position, row, *maps)


def span_join_kernel(s_ref, own, far, out_ref):
    @pl.when(s_ref[0] // 2 == 0)
    def _():
        join_kernel(own, far, out_ref)

    @pl.when(s_ref[0] // 2 == 1)
    def _():
        join_kernel(far, own, out_ref)


def span_join(position, own, far):
    return pl.pallas_call(
        span_join_kernel,
        grid_spec=pltpu.PrefetchScalarGridSpec(
            num_scalar_prefetch=1, grid=(), in_specs=vmem(2), out_specs=vmem(1)[0]
        ),
        out_shape=jax.ShapeDtypeStruct(own.shape, BF),
        compiler_params=pltpu.CompilerParams(vmem_limit_bytes=VMEM_LIMIT),
        name="span_join",
    )(position, own, far)


def lead_kernel(leaders, early, s_ref, tm_ref, row_ref, direct_ref, *refs):
    sets, out_ref = (refs[:leaders], refs[leaders : 2 * leaders]), refs[2 * leaders]

    @pl.when(tm_ref[0] < early)
    def _():
        out_ref[...] = direct_ref[...]

    for mine in range(leaders):
        for late in range(2):
            reached = (tm_ref[0] > early) if late else (tm_ref[0] == early)

            @pl.when(jnp.logical_and(s_ref[0] // 2 == mine, reached))
            def _():
                current = row_ref[...]
                for p in range(mine):
                    current = apply_map(current, sets[late][p ^ mine])
                out_ref[...] = current


def lead(position, span, row, direct, maps, maps_late, early):
    leaders = len(maps)
    return pl.pallas_call(
        functools.partial(lead_kernel, leaders, early),
        grid_spec=pltpu.PrefetchScalarGridSpec(
            num_scalar_prefetch=2,
            grid=(),
            in_specs=vmem(2 + 2 * leaders),
            out_specs=vmem(1)[0],
        ),
        out_shape=jax.ShapeDtypeStruct(row.shape, F32),
        compiler_params=pltpu.CompilerParams(vmem_limit_bytes=VMEM_LIMIT),
        name="lead",
    )(position, span, row, direct, *maps, *maps_late)


def sweep_kernel(leader, pieces, parts, s_ref, tm_ref, *refs):
    if leader:
        own_ref, first_map, first_vec, map_ref = refs[:4]
        refs = refs[4:]
    else:
        told_ref, refs = refs[0], refs[1 + parts :]
    stages, outs = refs[:pieces], refs[pieces : pieces + parts]
    current_ref, spread = refs[pieces + parts :]
    s = s_ref[0]

    @pl.when(s % 2 == int(leader))
    def _():
        if leader:

            @pl.when(tm_ref[0] == 0)
            def _():
                current_ref[...] = apply_map(own_ref[...], first_map) + first_vec[...]

            @pl.when(tm_ref[0] > 0)
            def _():
                current_ref[...] = apply_map(own_ref[...], map_ref)

            entry = current_ref[...]
        else:
            entry = told_ref[...]
        at = 0
        width = spread.shape[2]
        for p in range(pieces):
            for j in range(stages[p].shape[0]):
                mean = apply_map(entry, stages[p].at[j])
                for d in range(parts):
                    spread[d, at : at + 1, :] = mean[:, d * width : (d + 1) * width]
                at += 1
        for d in range(parts):
            outs[d][...] = spread[s ^ d]


def sweep(position, span, entry, stages, parts, even=(), filled=()):
    ns = entry.shape[1]
    pieces = len(stages)
    chunk = sum(x.shape[0] for x in stages)
    width = ns // parts
    leader = bool(even)
    return pl.pallas_call(
        functools.partial(sweep_kernel, leader, pieces, parts),
        grid_spec=pltpu.PrefetchScalarGridSpec(
            num_scalar_prefetch=2,
            grid=(),
            in_specs=vmem(1 + len(even) + len(filled) + pieces),
            out_specs=vmem(parts),
            scratch_shapes=[
                pltpu.VMEM((1, ns), F32),
                pltpu.VMEM((parts, chunk, width), F32),
            ],
        ),
        out_shape=[jax.ShapeDtypeStruct((chunk, width), F32)] * parts,
        input_output_aliases={3 + n: n for n in range(len(filled))},
        compiler_params=pltpu.CompilerParams(vmem_limit_bytes=VMEM_LIMIT),
        name="sweep_lead" if leader else "sweep",
    )(position, span, entry, *even, *filled, *stages)


def gather_kernel(parts, s_ref, *refs):
    blocks, out_ref = refs[:parts], refs[parts]
    rows = blocks[0].shape[0]
    for d in range(parts):
        out_ref[pl.ds(pl.multiple_of((s_ref[0] ^ d) * rows, rows), rows), :] = blocks[d][...]


def gather(position, blocks):
    rows, width = blocks[0].shape
    parts = len(blocks)
    return pl.pallas_call(
        functools.partial(gather_kernel, parts),
        grid_spec=pltpu.PrefetchScalarGridSpec(
            num_scalar_prefetch=1, grid=(), in_specs=vmem(parts), out_specs=vmem(1)[0]
        ),
        out_shape=jax.ShapeDtypeStruct((parts * rows, width), F32),
        compiler_params=pltpu.CompilerParams(vmem_limit_bytes=VMEM_LIMIT),
        name="gather",
    )(position, *blocks)


PIECES = 5


def piece_sizes(chunk):
    base, more = divmod(chunk - 2, PIECES - 2)
    return [1] + [base + 1] * more + [base] * (PIECES - 2 - more) + [1]


def means(dyn_cols, dyn_vals, obs_blocks, obs_op, obs_counts, obs_values, gain, sources, prior):
    steps, _, _, _ = dyn_vals.shape
    parts = lax.axis_size("state")
    spans = lax.axis_size("tm")
    chunk = steps // parts
    ns = prior.shape[0]
    s = lax.axis_index("state")
    t = lax.axis_index("tm")
    position = s.reshape(1).astype(jnp.int32)
    span = t.reshape(1).astype(jnp.int32)
    prior_row = prior.reshape(1, ns)

    def across(x, d):
        return lax.ppermute(x, "state", [(i, i ^ d) for i in range(parts)])

    def send(x, pairs):
        return lax.ppermute(x, ("tm", "state"), [(a * parts + b, c * parts + e) for (a, b), (c, e) in pairs])

    order = sorted(range(1, parts), reverse=True)
    sizes = piece_sizes(chunk)
    firsts = [sum(sizes[:n]) for n in range(len(sizes))]
    vals_far = pltpu.with_memory_space_constraint(dyn_vals, pltpu.HBM)
    gain_far = pltpu.with_memory_space_constraint(gain, pltpu.HBM)
    pieces = []
    for n, (first, size) in enumerate(zip(firsts, sizes)):
        source_arrays = (vals_far, gain_far) if n == 0 else (dyn_vals, gain)
        table = (sources, dyn_cols.transpose(2, 1, 0)) if n == 1 else ()
        packed = pack(position, span, *source_arrays, parts, chunk, first, size, table)
        arrived = {0: packed[0]}
        for d in order:
            arrived[d] = across(packed[d], d)
        pieces.append([arrived[d] for d in range(parts)])
        if n == 1:
            small = {0: packed[parts]}
            for d in order:
                small[d] = across(packed[parts + d], d)
            small = [small[d] for d in range(parts)]

    plan = plan_of(small, obs_blocks.T, obs_counts.reshape(1, steps), chunk)
    state = None
    stages = []
    for first, size, data in zip(firsts, sizes, pieces):
        state = chunk_piece(
            position, span, plan, data, small, obs_op, obs_values, prior_row, state, chunk, first, size
        )
        stages.append(state[0])
    vec = state[1]
    chunk_map = state[0].reshape(state[0].shape[1:])

    leads = [2 * p + 1 for p in range(parts // 2)]
    to_lead = [((a, l - 1), (a, l)) for a in range(spans) for l in leads]
    map_even = send(chunk_map, [pair for pair in to_lead if pair[0][0] > 0])
    first_vec = send(vec, to_lead[:1])
    first_map = send(chunk_map, to_lead[1 : len(leads)])
    current = hop(first_vec, chunk_map)
    pair = join(map_even, chunk_map)

    early = min(2, spans - 1)
    maps, maps_late = [pair], [pair]
    for d in range(2, parts, 2):
        pairs = [((a, l), (a, l ^ d)) for a in range(early, spans) for l in leads]
        maps.append(send(pair, pairs[: len(leads)]))
        maps_late.append(send(pair, pairs[len(leads) :]))

    direct = jnp.zeros((1, ns), F32)
    entry = jnp.zeros((1, ns), F32)
    for g in range(early):
        held = (pair,) if g > 0 else (first_map, chunk_map)
        for p in range(1, len(leads)):
            arriving = send(current, [((g, leads[p - 1]), (g, leads[p]))])
            direct = direct + arriving
            current = hop(arriving, *held)
        if g + 1 < early:
            arriving = send(current, [((g, leads[-1]), (g + 1, leads[0]))])
            direct = direct + arriving
            current = hop(arriving, pair)
        else:
            for l in leads:
                entry = entry + send(current, [((g, leads[-1]), (g + 1, l))])

    arriving = entry
    joined = span_join(position, *maps_late) if len(leads) == 2 else None
    for h in range(early, spans - 1):
        if h < early + 2 or joined is None:
            current = span_hop(position, arriving, maps if h == early else maps_late)
        else:
            current = hop(arriving, joined)
        arriving = send(current, [((h, l), (h + 1, l)) for l in leads])
        entry = entry + arriving

    own = lead(position, span, entry, direct, maps, maps_late, early)
    told = send(own, [(b, a) for a, b in to_lead])
    filled = sweep(position, span, own, stages, parts, even=(first_map, first_vec, map_even))
    mine = sweep(position, span, told, stages, parts, filled=filled)
    got = {0: mine[0]}
    for d in order:
        got[d] = across(mine[d], d)
    return gather(position, [got[d] for d in range(parts)])


def solution(mesh):
    return jax.shard_map(
        means,
        mesh=mesh,
        in_specs=(
            P("tm", "state", None),
            P("tm", "state", None, None),
            P("tm", None),
            P("tm", None, None),
            P("tm"),
            P("tm", None),
            P("tm", "state", None),
            P("tm", "state"),
            P(),
        ),
        out_specs=P("tm", "state"),
        check_vma=False,
    )
```
